256 devices in a mesh: row: 32 (over z, y), col: 8 (over x, core).
Axes of the slice: x: 4, y: 4, z: 8, core: 2. Of those that a mesh axis runs over, the one named last changes fastest.
Arguments:
- inputs: bfloat16 [1024, 12288], P('row', 'col'), may hold values from -6 to 6
- hidden_pre: bfloat16 [1024, 24576], P(None, 'row'), may hold values from -8 to 8
- out_grad: bfloat16 [1024, 12288], P('row', 'col'), may hold values from -6 to 6
- weight_in: bfloat16 [12288, 24576], P('col', 'row'), may hold values from -0.0546875 to 0.0546875
- weight_out: bfloat16 [24576, 12288], P('row', 'col'), may hold values from -0.0390625 to 0.0390625
Outputs:
- grad_in: bfloat16 [1024, 12288], P('row', 'col')
- grad_weight_in: bfloat16 [12288, 24576], P('col', 'row')
- grad_weight_out: bfloat16 [24576, 12288], P('row', 'col')
The draws below stay inside these ranges and needn't reach their ends.
All inputs are finite; a program needn't handle non-finite values.
Results may differ from the reference program's by a relative error of at most 0.0049.
Values may be sent and summed in bfloat16 or wider, within the bound.
A program may use at most 128 MiB of HBM per device.

```python
import jax
import jax.numpy as jnp

D = 12288
FF = 24576
TOKENS = 1024


def level_of(rng, shape, shards, low, top_value):
    gain, own = 1.0, jax.random.fold_in(rng, 6)
    for dim, blocks in shards:
        draws = jnp.exp(jax.random.uniform(jax.random.fold_in(own, dim), (blocks,), jnp.float32, low / len(shards), top_value / len(shards)))
        gain = gain * jnp.repeat(draws, shape[dim] // blocks).reshape([-1 if axis == dim else 1 for axis in range(len(shape))])
    return gain


def normal_values(stream_key, dims, width, reach, pieces=(), kind=jnp.bfloat16):
    drawn = jax.random.normal(stream_key, dims, jnp.float32) * width
    if len(pieces) > 0:
        drawn = level_of(stream_key, dims, pieces, -0.22, 0.18) * drawn
    return jnp.clip(drawn, min=-reach, max=reach).astype(kind)


def setup_inputs(seed: int = 0) -> dict:
    seeds = jax.random.split(jax.random.key(seed), 6)
    inputs = normal_values(seeds[0], (TOKENS, D), 1.0, 6.0, ((0, 32), (1, 8)))
    hidden_pre = normal_values(seeds[1], (TOKENS, FF), 1.5, 8.0, ((1, 32),))
    out_grad = normal_values(seeds[2], (TOKENS, D), 1.0, 6.0, ((0, 32), (1, 8)))
    weight_in = normal_values(seeds[3], (D, FF), D ** -0.5, 0.0546875, ((0, 8), (1, 32)))
    weight_out = normal_values(seeds[4], (FF, D), FF ** -0.5, 0.0390625, ((0, 32), (1, 8)))
    return {"inputs": inputs, "hidden_pre": hidden_pre, "out_grad": out_grad, "weight_in": weight_in, "weight_out": weight_out}


def gelu_parts(hidden_pre):
    hval = hidden_pre.astype(jnp.float32)
    inner = 0.7978845608 * (hval + 0.044715 * hval * hval * hval)
    tval = jnp.tanh(inner)
    act = 0.5 * hval * (1.0 + tval)
    slope = 0.5 * (1.0 + tval) + 0.5 * hval * (1.0 - tval * tval) * 0.7978845608 * (1.0 + 3.0 * 0.044715 * hval * hval)
    return act, slope


def reference(inputs, hidden_pre, out_grad, weight_in, weight_out):
    act, slope = gelu_parts(hidden_pre)
    act_b = act.astype(jnp.bfloat16)
    d_act = jnp.dot(out_grad, weight_out.T, preferred_element_type=jnp.float32)
    d_hid = (d_act * slope).astype(jnp.bfloat16)
    grad_weight_out = jnp.dot(act_b.T, out_grad, preferred_element_type=jnp.float32).astype(jnp.bfloat16)
    grad_in = jnp.dot(d_hid, weight_in.T, preferred_element_type=jnp.float32).astype(jnp.bfloat16)
    grad_weight_in = jnp.dot(inputs.T, d_hid, preferred_element_type=jnp.float32).astype(jnp.bfloat16)
    return grad_in, grad_weight_in, grad_weight_out
```

```python
import functools

import jax
import jax.numpy as jnp
from jax import lax
from jax.experimental import pallas as pl
from jax.experimental.pallas import tpu as pltpu
from jax.sharding import PartitionSpec as P

MESH = pl.DeviceIdType.MESH
F32, BF16 = jnp.float32, jnp.bfloat16
NT = (((1,), (1,)), ((), ()))
TN = (((0,), (0,)), ((), ()))
NN = (((1,), (0,)), ((), ()))


def gelu_terms(h):
    u = 0.7978845608 * (h + 0.044715 * h * h * h)
    return jnp.tanh(u)


def kernel(dims, inp, hid, grad, w_in, w_out, g_in, gw_in, gw_out,
           G, I, H, WI, WO, AT, D, PR, XS, XR, DH, PF, AS, AR, YB, YR, BS, BR, YA, AY, OUT, GI, GO,
           loc, out_sem, s_yo, r_yo, s_z, r_z, s_by, r_by, s_x, r_x):
    NZ, NY, NX, T, W, F = dims
    HOPS = NZ // 2
    QW = W // 4
    HW = W // 2
    row, col = lax.axis_index("row"), lax.axis_index("col")
    z, y = row // NY, row % NY
    x, c = col // 2, col % 2

    def zdev(sign):
        return (((z + sign + NZ) % NZ) * NY + y, col)

    def ydev(j):
        return (z * NY + (y + j) % NY, col)

    def xdev(j):
        return (row, ((x + j) % NX) * 2 + c)

    partner = (row, x * 2 + 1 - c)
    SIGN = (1, -1)

    def zoff(k):
        return (z + k + 2 * NZ) % NZ

    def yoff(k):
        return (y + k + 2 * NY) % NY

    def xoff(k):
        return (x + k + 2 * NX) % NX

    def limit(d, q):
        return HOPS if (q % 2 == 0) == (d == 0) else HOPS - 1

    def qs(q):
        return pl.ds(q * QW, QW)

    B = pl.ds(HW, HW)
    A = pl.ds(0, HW)

    def rcopy(src, dst, ssem, rsem, dev):
        return pltpu.make_async_remote_copy(src_ref=src, dst_ref=dst, send_sem=ssem, recv_sem=rsem,
                                            device_id=dev, device_id_type=MESH)

    sent = []

    def send(src, dst, ssem, rsem, dev):
        cp = rcopy(src, dst, ssem, rsem, dev)
        cp.start()
        sent.append(cp)

    def arrived(region, ssem, rsem, dev):
        rcopy(region, region, ssem, rsem, dev).wait_recv()

    def zi(p, d, q, h):
        return ((p * 2 + d) * 4 + q) * HOPS + h - 1

    loads = [
        pltpu.make_async_copy(grad, G.at[z, y], loc.at[0]),
        pltpu.make_async_copy(inp, I.at[z, y], loc.at[1]),
        pltpu.make_async_copy(hid, H, loc.at[2]),
        pltpu.make_async_copy(w_out, WO, loc.at[3]),
        pltpu.make_async_copy(w_in, WI, loc.at[4]),
    ]
    for cp in loads:
        cp.start()

    barrier = pltpu.get_barrier_semaphore()
    peers = [zdev(1), zdev(-1)] if NZ > 2 else [zdev(1)]
    peers += [ydev(j) for j in range(1, NY)] + [xdev(j) for j in range(1, NX)] + [partner]
    for dev in peers:
        pl.semaphore_signal(barrier, inc=1, device_id=dev, device_id_type=MESH)
    pl.semaphore_wait(barrier, len(peers))

    def gather(p, own, buf, load):
        NJ = NY - 1
        for j in range(1, NY):
            i = p * NJ + j - 1
            send(own, buf.at[z, y], s_yo.at[i], r_yo.at[i], ydev(j))
        for q in (2, 3):
            for d in (0, 1):
                if limit(d, q) >= 1:
                    i = zi(p, d, q, 1)
                    send(own.at[:, qs(q)], buf.at[z, y, :, qs(q)], s_z.at[i], r_z.at[i], zdev(SIGN[d]))
        yield
        load.wait()
        for j in range(1, NY):
            i = p * NJ + j - 1
            arrived(buf.at[z, yoff(-j)], s_yo.at[i], r_yo.at[i], ydev(j))
        for q in (0, 1):
            for d in (0, 1):
                if limit(d, q) >= 1:
                    i = zi(p, d, q, 1)
                    reg = buf.at[z, :, :, qs(q)]
                    send(reg, reg, s_z.at[i], r_z.at[i], zdev(SIGN[d]))
        yield
        for h in range(1, HOPS + 1):
            for pair in ((2, 3), (0, 1)):
                for q in pair:
                    for d in (0, 1):
                        if h > limit(d, q):
                            continue
                        zb = zoff(-SIGN[d] * h)
                        reg = buf.at[zb, y, :, qs(q)] if q >= 2 else buf.at[zb, :, :, qs(q)]
                        i = zi(p, d, q, h)
                        arrived(reg, s_z.at[i], r_z.at[i], zdev(SIGN[d]))
                        if h < limit(d, q):
                            i = zi(p, d, q, h + 1)
                            send(reg, reg, s_z.at[i], r_z.at[i], zdev(SIGN[d]))
                if pair == (2, 3):
                    for k in ((h, NZ - h) if h < HOPS else (h,)):
                        reg = buf.at[zoff(k), y, :, B]
                        for j in range(1, NY):
                            i = (p * NZ + k) * NJ + j - 1
                            send(reg, reg, s_by.at[i], r_by.at[i], ydev(j))
                yield
        for h in range(1, HOPS + 1):
            for k in ((h, NZ - h) if h < HOPS else (h,)):
                for j in range(1, NY):
                    i = (p * NZ + k) * NJ + j - 1
                    arrived(buf.at[zoff(k), yoff(-j), :, B], s_by.at[i], r_by.at[i], ydev(j))
            yield

    BT = NY * T

    def act_piece(i):
        h = H[pl.ds(pl.multiple_of(i * BT, BT), BT), :].astype(F32)
        t = gelu_terms(h)
        a = (0.5 * h * (1.0 + t)).astype(BF16)
        AT[:, pl.ds(pl.multiple_of(i * BT, BT), BT)] = a.T

    NTILE = 256

    def d_act_piece(i, xp):
        lhs = G[pl.ds(2 * xp, 2)].reshape(2 * BT, W)

        @pl.loop(0, F // NTILE)
        def _(n):
            cols = pl.ds(pl.multiple_of(n * NTILE, NTILE), NTILE)
            r = lax.dot_general(lhs, WO[cols, :], NT, preferred_element_type=F32)
            D[i, :, :, cols] = r.reshape(2, BT, NTILE)

    def gwo_piece(n):
        cols = pl.ds(pl.multiple_of(n * NTILE, NTILE), NTILE)
        rhs = G[:, :, :, cols].reshape(NZ * BT, NTILE)
        GO[:, cols] = lax.dot_general(AT[...], rhs, NN, preferred_element_type=F32).astype(BF16)

    def gwi_piece(n):
        cols = pl.ds(pl.multiple_of(n * NTILE, NTILE), NTILE)
        lhs = I[:, :, :, cols].reshape(NZ * BT, NTILE)
        GI[cols, :] = lax.dot_general(lhs, DH[...].reshape(NZ * BT, F), TN, preferred_element_type=F32).astype(BF16)

    def p_piece(blocks):
        vals = [DH[b] for b in blocks]
        lhs = vals[0] if len(vals) == 1 else jnp.concatenate(vals, axis=0)

        @pl.loop(0, W // NTILE)
        def _(n):
            cols = pl.ds(pl.multiple_of(n * NTILE, NTILE), NTILE)
            r = lax.dot_general(lhs, WI[cols, :], NT, preferred_element_type=F32)
            for m, b in enumerate(blocks):
                PF[b, :, :, cols] = r[m * BT:(m + 1) * BT].reshape(NY, T, NTILE)

    loads[2].wait()
    ag = gather(0, grad, G, loads[0])
    next(ag)
    done = 0
    for _ in ag:
        if done < NZ:
            act_piece(done)
            done += 1
    for i in range(done, NZ):
        act_piece(i)

    ag = gather(1, inp, I, loads[1])
    next(ag)
    step = lambda: next(ag, None)
    loads[3].wait()
    offs = {4: [2, 1, 3, 0], 2: [1, 0]}[NX]
    b_own = 2 * x + c

    def finish(i, off):
        k = i
        arrived(PR.at[i], s_x.at[k], r_x.at[k], partner)
        s = D[i, c] + PR[i]
        if off:
            XS[i] = s.astype(BF16)
            k = NX + i
            send(XS.at[i], XR.at[i], s_x.at[k], r_x.at[k], xdev(off))
            return
        for j in range(NX - 1):
            k = NX + j
            arrived(XR.at[j], s_x.at[k], r_x.at[k], xdev(offs[j]))
            s = s + XR[j].astype(F32)
        h = H[pl.ds(pl.multiple_of(b_own * BT, BT), BT), :].astype(F32)
        t = gelu_terms(h)
        slope = 0.5 * (1.0 + t) + 0.5 * h * (1.0 - t * t) * 0.7978845608 * (1.0 + 3.0 * 0.044715 * h * h)
        DH[b_own] = (s * slope).astype(BF16)
        reg = DH.at[b_own]
        for j in range(NX - 1):
            k = 2 * NX + j
            send(reg, reg, s_x.at[k], r_x.at[k], xdev(offs[j]))
        k = 3 * NX
        send(reg, reg, s_x.at[k], r_x.at[k], partner)

    for i, off in enumerate(offs):
        d_act_piece(i, xoff(off))
        send(D.at[i, 1 - c], PR.at[i], s_x.at[i], r_x.at[i], partner)
        step()
        if i > 0:
            finish(i - 1, offs[i - 1])
        step()
    n_go = W // NTILE
    go = 0
    while go < (n_go + 1) // 2:
        gwo_piece(go)
        go += 1
        step()
    finish(NX - 1, 0)
    step()
    while go < n_go:
        gwo_piece(go)
        go += 1
        step()
    go_out = pltpu.make_async_copy(GO, gw_out, out_sem.at[0])
    go_out.start()
    for j in (1, 0, 2) if NX == 4 else (0,):
        off = offs[j]
        k = 2 * NX + j
        reg = DH.at[2 * xoff(-off) + c]
        arrived(reg, s_x.at[k], r_x.at[k], xdev(off))
        k = 3 * NX + 1 + j
        send(reg, reg, s_x.at[k], r_x.at[k], partner)
        step()
    k = 3 * NX
    arrived(DH.at[2 * x + 1 - c], s_x.at[k], r_x.at[k], partner)
    for j in (1, 0, 2) if NX == 4 else (0,):
        k = 3 * NX + 1 + j
        arrived(DH.at[2 * xoff(-offs[j]) + 1 - c], s_x.at[k], r_x.at[k], partner)
    for _ in ag:
        pass

    loads[4].wait()
    NJ = NY - 1
    p = 2

    def rs_first(d):
        blocks = [zoff(d)] if d in (0, HOPS) else [zoff(d), zoff(-d)]
        p_piece(blocks)
        for k in ((d,) if d in (0, HOPS) else (d, NZ - d)):
            zb = zoff(k)
            YB[zb] = PF[zb, :, :, B].astype(BF16)
            for j in range(1, NY):
                i = (p * NZ + k) * NJ + j - 1
                send(YB.at[zb, yoff(j)], YR.at[k, j - 1], s_by.at[i], r_by.at[i], ydev(j))

    def rs_a(d):
        for q in (0, 1):
            for dr in (0, 1):
                if d > limit(dr, q):
                    continue
                v = PF[zoff(SIGN[dr] * d), :, :, qs(q)]
                if d + 1 <= limit(dr, q):
                    i = zi(p, dr, q, d + 1)
                    m = zi(0, dr, q, d + 1)
                    arrived(AR.at[m], s_z.at[i], r_z.at[i], zdev(SIGN[dr]))
                    v = v + AR[m].astype(F32)
                i = zi(p, dr, q, d)
                m = zi(0, dr, q, d)
                AS[m] = v.astype(BF16)
                send(AS.at[m], AR.at[m], s_z.at[i], r_z.at[i], zdev(SIGN[dr]))

    def y_sum(k):
        for j in range(1, NY):
            i = (p * NZ + k) * NJ + j - 1
            arrived(YR.at[k, j - 1], s_by.at[i], r_by.at[i], ydev(j))
        v = PF[zoff(k), y, :, B]
        for j in range(1, NY):
            v = v + YR[k, j - 1].astype(F32)
        return v

    def rs_b(d):
        for k in ((d,) if d in (0, HOPS) else (d, NZ - d)):
            v = y_sum(k)
            for q in (2, 3):
                vq = v[:, (q - 2) * QW:(q - 1) * QW]
                if d == 0:
                    for dr in (0, 1):
                        if limit(dr, q) >= 1:
                            i = zi(p, dr, q, 1)
                            m = zi(0, dr, q - 2, 1)
                            arrived(BR.at[m], s_z.at[i], r_z.at[i], zdev(SIGN[dr]))
                            vq = vq + BR[m].astype(F32)
                    OUT[:, qs(q)] = vq.astype(BF16)
                    continue
                for dr in (0, 1):
                    if d > limit(dr, q) or (k != d if dr == 0 else k != NZ - d):
                        continue
                    if d + 1 <= limit(dr, q):
                        i = zi(p, dr, q, d + 1)
                        m = zi(0, dr, q - 2, d + 1)
                        arrived(BR.at[m], s_z.at[i], r_z.at[i], zdev(SIGN[dr]))
                        vs = vq + BR[m].astype(F32)
                    else:
                        vs = vq
                    i = zi(p, dr, q, d)
                    m = zi(0, dr, q - 2, d)
                    BS[m] = vs.astype(BF16)
                    send(BS.at[m], BR.at[m], s_z.at[i], r_z.at[i], zdev(SIGN[dr]))

    gi = 0
    n_gi = W // NTILE
    for d in range(HOPS, -1, -1):
        rs_first(d)
        if d >= 1:
            rs_a(d)
        if d + 1 <= HOPS:
            rs_b(d + 1)
        if d < HOPS and gi < n_gi:
            gwi_piece(gi)
            gi += 1
    for q in (0, 1):
        v = PF[z, :, :, qs(q)]
        for dr in (0, 1):
            if limit(dr, q) >= 1:
                i = zi(p, dr, q, 1)
                m = zi(0, dr, q, 1)
                arrived(AR.at[m], s_z.at[i], r_z.at[i], zdev(SIGN[dr]))
                v = v + AR[m].astype(F32)
        PF[z, :, :, qs(q)] = v
        YA[:, :, qs(q)] = v.astype(BF16)
    for j in range(1, NY):
        i = p * NJ + j - 1
        send(YA.at[yoff(j)], AY.at[j - 1], s_yo.at[i], r_yo.at[i], ydev(j))
    while gi < n_gi:
        gwi_piece(gi)
        gi += 1
    gi_out = pltpu.make_async_copy(GI, gw_in, out_sem.at[1])
    gi_out.start()
    rs_b(0)
    v = PF[z, y, :, A]
    for j in range(1, NY):
        i = p * NJ + j - 1
        arrived(AY.at[j - 1], s_yo.at[i], r_yo.at[i], ydev(j))
        v = v + AY[j - 1].astype(F32)
    OUT[:, A] = v.astype(BF16)
    in_out = pltpu.make_async_copy(OUT, g_in, out_sem.at[2])
    in_out.start()
    for cp in sent:
        cp.wait_send()
    go_out.wait()
    gi_out.wait()
    in_out.wait()


def build(dims):
    NZ, NY, NX, T, W, F = dims
    HOPS, BT, NJ = NZ // 2, NY * T, NY - 1

    def body(inputs, hidden_pre, out_grad, weight_in, weight_out):
        any_spec = pl.BlockSpec(memory_space=pl.ANY)
        vm = pltpu.VMEM
        nz_sem = 3 * 2 * 4 * HOPS
        dma = pltpu.SemaphoreType.DMA
        return pl.pallas_call(
            functools.partial(kernel, dims),
            out_shape=(
                jax.ShapeDtypeStruct((T, W), BF16),
                jax.ShapeDtypeStruct((W, F), BF16),
                jax.ShapeDtypeStruct((F, W), BF16),
            ),
            in_specs=[any_spec] * 5,
            out_specs=(any_spec,) * 3,
            scratch_shapes=[
                vm((NZ, NY, T, W), BF16),
                vm((NZ, NY, T, W), BF16),
                vm((NZ * BT, F), BF16),
                vm((W, F), BF16),
                vm((F, W), BF16),
                vm((F, NZ * BT), BF16),
                vm((NX, 2, BT, F), F32),
                vm((NX, BT, F), F32),
                vm((NX - 1, BT, F), BF16),
                vm((NX - 1, BT, F), BF16),
                vm((NZ, BT, F), BF16),
                vm((NZ, NY, T, W), F32),
                vm((2 * 4 * HOPS, NY, T, W // 4), BF16),
                vm((2 * 4 * HOPS, NY, T, W // 4), BF16),
                vm((NZ, NY, T, W // 2), BF16),
                vm((NZ, NJ, T, W // 2), BF16),
                vm((2 * 4 * HOPS, T, W // 4), BF16),
                vm((2 * 4 * HOPS, T, W // 4), BF16),
                vm((NY, T, W // 2), BF16),
                vm((NJ, T, W // 2), BF16),
                vm((T, W), BF16),
                vm((W, F), BF16),
                vm((F, W), BF16),
                dma((5,)),
                dma((3,)),
                dma((3 * NJ,)), dma((3 * NJ,)),
                dma((nz_sem,)), dma((nz_sem,)),
                dma((3 * NZ * NJ,)), dma((3 * NZ * NJ,)),
                dma((4 * NX,)), dma((4 * NX,)),
            ],
            compiler_params=pltpu.CompilerParams(
                collective_id=0, has_side_effects=True, vmem_limit_bytes=60 * 2**20
            ),
        )(inputs, hidden_pre, out_grad, weight_in, weight_out)

    return body


def solution(mesh):
    return jax.shard_map(
        build((8, 4, 4, 32, 1536, 768)),
        mesh=mesh,
        in_specs=(
            P("row", "col"),
            P(None, "row"),
            P("row", "col"),
            P("col", "row"),
            P("row", "col"),
        ),
        out_specs=(P("row", "col"), P("col", "row"), P("row", "col")),
        check_vma=False,
    )
```

```python
import functools

import jax
import jax.numpy as jnp
from jax import lax
from jax.experimental import pallas as pl
from jax.experimental.pallas import tpu as pltpu
from jax.sharding import PartitionSpec as P

MESH = pl.DeviceIdType.MESH
F32, BF16 = jnp.float32, jnp.bfloat16
NT = (((1,), (1,)), ((), ()))
TN = (((0,), (0,)), ((), ()))
NN = (((1,), (0,)), ((), ()))
NTILE = 256
SIGN = (1, -1)

RATE = 45500.0
CORE_RATE = 650000.0
HOP, HOP2 = 2.4, 0.65
CORE_HOP = 1.0
PRIO1 = 0.6
GATE_Y, GATE_B, GATE_BY = ("arr", 0, 0, 0, 4, 2), ("By", 0, 3), ("By", 0, 4)


class Task:
    def __init__(self, name, deps=(), waits=(), sends=(), cost=0.05, prio=1, run=None):
        self.name, self.deps, self.waits, self.sends = name, tuple(deps), tuple(waits), tuple(sends)
        self.cost, self.prio, self.run = cost, prio, run


class Msg:
    def __init__(self, name, index, links, nbytes, make, region):
        self.name, self.index, self.links, self.nbytes = name, index, links, nbytes
        self.make, self.region = make, region


def order_of(tasks, msgs, loads):
    free = {}
    arrive = dict(loads)
    done, now, out = {}, 0.0, []
    left = list(tasks)
    while left:
        best, soonest = None, None
        for i, t in enumerate(left):
            if any(d not in done for d in t.deps) or any(w not in arrive for w in t.waits):
                continue
            ready = max([0.0] + [arrive[w] for w in t.waits])
            key = (t.prio, ready, i)
            if ready <= now and (best is None or key < best[0]):
                best = (key, i)
            if soonest is None or ready < soonest[0]:
                soonest = (ready, i)
        if best is None:
            now = max(now, soonest[0])
            continue
        t = left.pop(best[1])
        now += t.cost
        done[t.name] = now
        out.append(t)
        for m in t.sends:
            m = msgs[m]
            if m.links == ("core",):
                start = max(now, free.get("core", 0.0))
                free["core"] = start + m.nbytes / CORE_RATE
                arrive[m.name] = free["core"] + CORE_HOP
            else:
                end = 0.0
                for link in m.links:
                    free[link] = max(now, free.get(link, 0.0)) + m.nbytes / RATE
                    end = max(end, free[link])
                arrive[m.name] = end + HOP + (HOP2 if len(m.links) > 1 else 0.0)
    return out, now, done, arrive, free


def gelu_tanh(h):
    return jnp.tanh(0.7978845608 * (h + 0.044715 * h * h * h))


def plan(dims, pos, r):
    NZ, NY, NX, T, W, F, bounds, NA = dims
    NQ = len(bounds) - 1
    z, y, x, c = pos
    HOPS, BT, XT, FH, WH = NZ // 2, NY * T, NY * T // NX, F // 2, W // 2
    tasks, msgs = [], {}

    def task(name, **kw):
        tasks.append(Task(name, **kw))
        return name

    def msg(name, links, nbytes, make, region):
        msgs[name] = Msg(name, len(msgs), links, nbytes, make, region)
        return name

    def qs(q):
        return pl.ds(bounds[q], bounds[q + 1] - bounds[q])

    def qw(q):
        return bounds[q + 1] - bounds[q]

    def mod(v, n):
        return (v + 4 * n) % n

    def zdev(s):
        return {"row": mod(z + s, NZ) * NY + y}

    def ydev(s):
        return {"row": z * NY + mod(y + s, NY)}

    def xdev(s):
        return {"col": mod(x + s, NX) * 2 + c}

    core = {"col": x * 2 + 1 - c}
    zof, yof, xof = (lambda k: mod(z + k, NZ)), (lambda k: mod(y + k, NY)), (lambda k: mod(x + k, NX))
    ZL, YL = ("z+", "z-"), ("y+", "y-")

    def xlinks(j):
        return ("x+",) if j == 1 else ("x-",) if j == NX - 1 else ("x+", "x-")

    A, B = pl.ds(0, bounds[NA]), pl.ds(bounds[NA], W - bounds[NA])
    AW, BW = bounds[NA], W - bounds[NA]
    mid = bounds[NA // 2]
    GA = (pl.ds(0, mid), pl.ds(mid, AW - mid))
    GB = (qs(NA), qs(NA + 1))
    QA, QB = tuple(range(NA)), (NA, NA + 1)
    YD = ((1, 0), (3, 1), (2, None))

    def half(v):
        return pl.ds(pl.multiple_of(v * FH, 128), FH)

    def limit(d, q):
        return HOPS if (q % 2 == 0) == (d == 0) else HOPS - 1

    def chains(q):
        return [(d, h) for d in (0, 1) for h in range(1, limit(d, q) + 1)]

    def gather(p, own, buf, gate_y, gate_b, gate_by):
        ld = ("load", p)
        for j, d in YD:
            msg(("yo", p, j), YL if d is None else (YL[d],), T * AW * 2,
                lambda j=j: (r[own].at[:, A], r[buf].at[z, y, :, A], ydev(j)), lambda j=j: r[buf].at[z, yof(-j), :, A])
        yo = [("yo", p, j) for j in (1, 3, 2)]
        task(("y", p), deps=gate_y, sends=yo, prio=0)
        for i in range(4):
            for q in (0, 1):
                cols = pl.ds(q * WH, WH) if i == 0 else GA[q]
                pick = lambda b, i=i, cols=cols: r[buf].at[b, yof(-i), :, cols]
                for d, h in chains(q):
                    s = SIGN[d]
                    zb = lambda k, s=s: zof(-s * k)
                    if i == 0 and h == 1:
                        make = lambda s=s, pick=pick, cols=cols: (r[own].at[:, cols], pick(z), zdev(s))
                    else:
                        make = lambda h=h, s=s, pick=pick, zb=zb: (pick(zb(h - 1)), pick(zb(h - 1)), zdev(s))
                    msg(("gz", p, d, q, h, i), (ZL[d],), T * cols.size * 2, make, lambda h=h, pick=pick, zb=zb: pick(zb(h)))
                    nxt = [("gz", p, d, q, h + 1, i)] if h < limit(d, q) else []
                    dep = ("arr", p, d, q, h - 1, i) if h > 1 else ("zA", p, i) if i else ("zB", p)
                    task(("arr", p, d, q, h, i), waits=[("gz", p, d, q, h, i)], sends=nxt, prio=0 + p * PRIO1, deps=[dep])
        first = lambda i: [("gz", p, d, q, 1, i) for q in (0, 1) for d in (0, 1) if limit(d, q) >= 1]
        task(("zB", p), deps=gate_b, sends=first(0), prio=0)
        for i in (1, 3, 2):
            task(("zA", p, i), deps=[("y", p)], waits=[("yo", p, i)], sends=first(i), prio=0)
        for k in range(NZ):
            come = [[], []]
            for i in range(4 if k else 0):
                for q in (0, 1):
                    at = ("arr", p, 1, q, k, i) if k <= limit(1, q) else ("arr", p, 0, q, NZ - k, i)
                    come[i > 0].append(at)
            for d in (0, 1):
                s = SIGN[d]
                msg(("by", p, k, d), (YL[d],), T * BW * 2,
                    lambda s=s, k=k: (r[buf].at[zof(k), y, :, B] if k else r[own].at[:, B], r[buf].at[zof(k), y, :, B], ydev(s)),
                    lambda s=s, k=k: r[buf].at[zof(k), yof(-s), :, B])
                fwd = lambda s, k, cols: r[buf].at[zof(k), yof(-s), :, cols]
                cols = GB[d]
                msg(("byr", p, k, d), (YL[d],), T * cols.size * 2,
                    lambda s=s, k=k, cols=cols, fwd=fwd: (fwd(s, k, cols), fwd(s, k, cols), ydev(s)),
                    lambda k=k, cols=cols: r[buf].at[zof(k), yof(-2), :, cols])
            task(("By", p, k), deps=(come[0] if k else [("y", p)]) + gate_by,
                 sends=[("by", p, k, 0), ("by", p, k, 1)], prio=p * PRIO1)
            for d in (0, 1):
                task(("Byr", p, k, d), deps=[("By", p, k)], waits=[("by", p, k, d)], sends=[("byr", p, k, d)],
                     prio=p * PRIO1)
            task(("blk", p, k), deps=(come[1] if k else [("zA", p, i) for i in (1, 2, 3)]) + [("Byr", p, k, 0), ("Byr", p, k, 1)],
                 waits=[("byr", p, k, 0), ("byr", p, k, 1)] + ([] if k else [ld]), prio=p * PRIO1)

    gather(0, "grad", "G", [], [], [])
    known = {t.name for t in tasks}
    gates = [[g] if g in known else [("zB", 0)] for g in (GATE_Y, GATE_B, GATE_BY)]
    gather(1, "inp", "I", *gates)
    for i in range(2, 5):
        task(("ld", i), waits=[("load", i)], cost=0, prio=1)

    def dot_d(k):
        zb = zof(k)
        lhs = r["G"][zb].reshape(BT, W)

        @pl.loop(0, F // NTILE)
        def _(n):
            cols = pl.ds(pl.multiple_of(n * NTILE, NTILE), NTILE)
            v = lax.dot_general(lhs, r["WO"][cols, :], NT, preferred_element_type=F32)
            r["D"][zb, :, :, cols] = v.reshape(NX, XT, NTILE)

    def sum_core(k):
        r["XS"][k] = r["D"][zof(k), :, :, half(c)] + r["PR"][k]

    def make_dh(k):
        v = r["XS"][k, x]
        for j in range(1, NX):
            v = v + r["XR"][k, j - 1]
        zb = zof(k)
        h = r["H"][pl.ds(pl.multiple_of(zb * BT + x * XT, XT), XT), half(c)].astype(F32)
        t = gelu_tanh(h)
        slope = 0.5 * (1.0 + t) + 0.5 * h * (1.0 - t * t) * 0.7978845608 * (1.0 + 3.0 * 0.044715 * h * h)
        r["DH"][zb, x, :, half(c)] = (v * slope).astype(BF16)

    for k in range(NZ):
        msg(("pair", k), ("core",), BT * FH * 4,
            lambda k=k: (r["D"].at[zof(k), :, :, half(1 - c)], r["PR"].at[k], core), lambda k=k: r["PR"].at[k])
        for j in range(1, NX):
            msg(("xs", k, j), xlinks(j), XT * FH * 4,
                lambda k=k, j=j: (r["XS"].at[k, xof(j)], r["XR"].at[k, j - 1], xdev(j)), lambda k=k, j=j: r["XR"].at[k, j - 1])
            msg(("dh", k, j), xlinks(j), XT * FH * 2,
                lambda k=k, j=j: (r["DH"].at[zof(k), x, :, half(c)], r["DH"].at[zof(k), x, :, half(c)], xdev(j)),
                lambda k=k, j=j: r["DH"].at[zof(k), xof(-j), :, half(c)])
        msg(("df", k), ("core",), BT * FH * 2,
            lambda k=k: (r["DH"].at[zof(k), :, :, half(c)], r["DH"].at[zof(k), :, :, half(c)], core),
            lambda k=k: r["DH"].at[zof(k), :, :, half(1 - c)])
        peers = range(1, NX)
        task(("d", k), deps=[("blk", 0, k), ("ld", 3)], sends=[("pair", k)], cost=1.2, prio=1, run=lambda k=k: dot_d(k))
        task(("s", k), deps=[("d", k)], waits=[("pair", k)], sends=[("xs", k, j) for j in peers], cost=0.3, prio=0.5,
             run=lambda k=k: sum_core(k))
        task(("h", k), deps=[("s", k), ("ld", 2)], waits=[("xs", k, j) for j in peers],
             sends=[("dh", k, j) for j in peers], cost=0.3, prio=0.5, run=lambda k=k: make_dh(k))
        task(("f", k), deps=[("h", k)], waits=[("dh", k, j) for j in peers], sends=[("df", k)], prio=0.5)
        task(("e", k), deps=[("f", k)], waits=[("df", k)], prio=0.5)

    def dot_p(k):
        zb = zof(k)
        lhs = r["DH"][zb].reshape(BT, F)

        @pl.loop(0, W // NTILE)
        def _(n):
            cols = pl.ds(pl.multiple_of(n * NTILE, NTILE), NTILE)
            v = lax.dot_general(lhs, r["WI"][cols, :], NT, preferred_element_type=F32)
            r["PF"][zb, :, :, cols] = v.reshape(NY, T, NTILE)

    def ystage(key, k, qq, dep, cost):
        slot = k
        off = bounds[qq[0]]
        loc = lambda q: pl.ds(bounds[q] - off, qw(q))

        def put(i, who, q, extra=None):
            v = r["PF"][zof(k), yof(who), :, qs(q)]
            if extra is not None:
                v = v + r["YR"][slot, extra, :, loc(q)].astype(F32)
            r["YS"][slot, i, :, loc(q)] = v.astype(BF16)

        for d in (0, 1):
            s, mine, other = SIGN[d], qq[d], qq[1 - d]
            for kind, q, i in (("r", mine, 0), ("n", mine, 1 + d), ("m", other, 1 + d)):
                mk = lambda i=i, q=q, s=s: (r["YS"].at[slot, i, :, loc(q)], r["YR"].at[slot, i, :, loc(q)], ydev(s))
                msg((kind, key, d), (YL[d],), T * qw(q) * 2, mk, lambda i=i, q=q: r["YR"].at[slot, i, :, loc(q)])

        def start():
            for d in (0, 1):
                put(0, 2, qq[d])
                put(1 + d, SIGN[d], qq[1 - d])

        task(("ys", key), deps=dep, sends=[("r", key, 0), ("r", key, 1), ("m", key, 0), ("m", key, 1)], cost=cost,
             prio=0.5, run=start)
        for d in (0, 1):
            task(("yc", key, d), deps=[("ys", key)], waits=[("r", key, d)], sends=[("n", key, d)], prio=0.3,
                 run=lambda d=d: put(1 + d, SIGN[d], qq[d], 0))

        def total():
            w = qw(qq[0]) + qw(qq[1])
            v = r["PF"][zof(k), y, :, pl.ds(off, w)]
            for i in (1, 2):
                v = v + r["YR"][slot, i, :, pl.ds(0, w)].astype(F32)
            return v

        return [(kind, key, d) for kind in ("n", "m") for d in (0, 1)], total

    order = [HOPS]
    for d in range(HOPS - 1, 0, -1):
        order += [d, NZ - d]
    order.append(0)
    tag = lambda q, d, h: (d * NA + q % NA) * HOPS + h - 1

    for q in range(NQ):
        for d, h in chains(q):
            s = SIGN[d]
            bs, br = ("AS", "AR") if q < NA else ("BS", "BR")
            cut = (lambda ref, m, q=q: ref.at[m, :, :, pl.ds(0, qw(q))]) if q < NA else (
                lambda ref, m, q=q: ref.at[m, :, pl.ds(0, qw(q))])
            m = tag(q, d, h)
            msg(("rz", d, q, h), (ZL[d],), (BT if q < NA else T) * qw(q) * 2,
                lambda m=m, s=s, bs=bs, br=br, cut=cut: (cut(r[bs], m), cut(r[br], m), zdev(s)),
                lambda m=m, br=br, cut=cut: cut(r[br], m))

    def step_a(d, q, h):
        v = r["PF"][zof(SIGN[d] * h), :, :, qs(q)]
        if h < limit(d, q):
            v = v + r["AR"][tag(q, d, h + 1), :, :, pl.ds(0, qw(q))].astype(F32)
        r["AS"][tag(q, d, h), :, :, pl.ds(0, qw(q))] = v.astype(BF16)

    def step_b(d, q, h, k):
        v = r["VB"][k, :, pl.ds(bounds[q] - bounds[NA], qw(q))]
        if h < limit(d, q):
            v = v + r["BR"][tag(q, d, h + 1), :, pl.ds(0, qw(q))].astype(F32)
        r["BS"][tag(q, d, h), :, pl.ds(0, qw(q))] = v.astype(BF16)

    for n, k in enumerate(order):
        task(("p", k), deps=[("e", k), ("ld", 4)], cost=1.2, prio=1 + 0.01 * n, run=lambda k=k: dot_p(k))
        waits, total = ystage(k, k, QB, [("p", k)], 0.2)

        def hold(k=k, total=total):
            r["VB"][k] = total()

        task(("v", k), deps=[("yc", k, 0), ("yc", k, 1)], waits=waits, cost=0.1, prio=0.4, run=hold)
        for q in range(NQ):
            for d, h in chains(q):
                if (h if d == 0 else NZ - h) != k:
                    continue
                waits = [("rz", d, q, h + 1)] if h < limit(d, q) else []
                dep = [("rzt", d, q, h + 1)] if h < limit(d, q) else []
                if q < NA:
                    task(("rzt", d, q, h), deps=dep + [("p", k)], waits=waits, sends=[("rz", d, q, h)], cost=0.12,
                         prio=0.3, run=lambda d=d, q=q, h=h: step_a(d, q, h))
                else:
                    task(("rzt", d, q, h), deps=dep + [("v", k)], waits=waits, sends=[("rz", d, q, h)], cost=0.05,
                         prio=0.3, run=lambda d=d, q=q, h=h, k=k: step_b(d, q, h, k))

    def last_a():
        for q in QA:
            v = r["PF"][z, :, :, qs(q)]
            for d in (0, 1):
                if limit(d, q) >= 1:
                    v = v + r["AR"][tag(q, d, 1), :, :, pl.ds(0, qw(q))].astype(F32)
            r["PF"][z, :, :, qs(q)] = v
            r["YA"][:, :, qs(q)] = v.astype(BF16)

    lasts = lambda qq: [("rz", d, q, 1) for q in qq for d in (0, 1) if limit(d, q) >= 1]
    sent = lambda qq: [("rzt",) + m[1:] for m in lasts(qq)]
    task("sumA", deps=[("p", 0)] + sent(QA), waits=lasts(QA), sends=[("ya", j) for j in (1, 3, 2)], cost=0.3, prio=0.3, run=last_a)
    for j, d in YD:
        msg(("ya", j), YL if d is None else (YL[d],), T * AW * 2,
            lambda j=j: (r["YA"].at[yof(j)], r["AY"].at[j - 1], ydev(j)), lambda j=j: r["AY"].at[j - 1])

    def out_a():
        v = r["PF"][z, y, :, A]
        for j in (1, 2, 3):
            v = v + r["AY"][j - 1].astype(F32)
        r["OUT"][:, A] = v.astype(BF16)

    task("outA", deps=["sumA"], waits=[("ya", j) for j in (1, 3, 2)], cost=0.1, prio=0.3, run=out_a)

    def out_b():
        for q in QB:
            v = r["VB"][0, :, pl.ds(bounds[q] - bounds[NA], qw(q))]
            for d in (0, 1):
                if limit(d, q) >= 1:
                    v = v + r["BR"][tag(q, d, 1), :, pl.ds(0, qw(q))].astype(F32)
            r["OUT"][:, qs(q)] = v.astype(BF16)

    task("outB", deps=[("v", 0)] + sent(QB), waits=lasts(QB), cost=0.1, prio=0.3, run=out_b)
    task("out", deps=["outA", "outB"], cost=0.05, run=lambda: r["store"](2))

    def act_piece(i):
        rows = pl.ds(i * BT, BT)
        h = r["H"][rows, :].astype(F32)
        r["AT"][:, rows] = (0.5 * h * (1.0 + gelu_tanh(h))).astype(BF16).T

    def gwo_piece(n):
        cols = pl.ds(n * NTILE, NTILE)
        rhs = r["G"][:, :, :, cols].reshape(NZ * BT, NTILE)
        r["GO"][:, cols] = lax.dot_general(r["AT"][...], rhs, NN, preferred_element_type=F32).astype(BF16)

    def gwi_piece(n):
        cols = pl.ds(n * NTILE, NTILE)
        lhs = r["I"][:, :, :, cols].reshape(NZ * BT, NTILE)
        rhs = r["DH"][...].reshape(NZ * BT, F)
        r["GI"][cols, :] = lax.dot_general(lhs, rhs, TN, preferred_element_type=F32).astype(BF16)

    for i in range(NZ):
        task(("act", i), deps=[("ld", 2)], cost=0.6, prio=5, run=lambda i=i: act_piece(i))
    for n in range(W // NTILE):
        task(("go", n), deps=[("blk", 0, k) for k in range(NZ)] + [("act", i) for i in range(NZ)], cost=0.9, prio=6,
             run=lambda n=n: gwo_piece(n))
    task("goout", deps=[("go", n) for n in range(W // NTILE)], prio=6, run=lambda: r["store"](0))
    for n in range(W // NTILE):
        task(("gi", n), deps=[("blk", 1, k) for k in range(NZ)] + [("e", k) for k in range(NZ)], cost=1.0, prio=7,
             run=lambda n=n: gwi_piece(n))
    task("giout", deps=[("gi", n) for n in range(W // NTILE)], prio=7, run=lambda: r["store"](1))
    return tasks, msgs


@functools.lru_cache(None)
def n_msgs(dims):
    return len(plan(dims, (0, 0, 0, 0), {})[1])


LOADS = {("load", 0): 0.5, ("load", 1): 0.5, ("load", 2): 1.5, ("load", 3): 3.0, ("load", 4): 4.5}
NAMES = ("inp", "hid", "grad", "w_in", "w_out", "g_in", "gw_in", "gw_out", "G", "I", "H", "WI", "WO", "AT", "D", "PR", "XS",
         "XR", "DH", "PF", "AS", "AR", "YS", "YR", "YA", "AY", "VB", "BS", "BR", "OUT", "GI", "GO", "loc", "osem", "ss", "rs")


def kernel(dims, *refs):
    NZ, NY, NX = dims[:3]
    r = dict(zip(NAMES, refs, strict=True))
    row, col = lax.axis_index("row"), lax.axis_index("col")
    z, y, x, c = row // NY, row % NY, col // 2, col % 2

    copies = [(r["grad"], r["G"].at[z, y]), (r["inp"], r["I"].at[z, y]), (r["hid"], r["H"]), (r["w_out"], r["WO"]),
              (r["w_in"], r["WI"])]
    copies = [pltpu.make_async_copy(a, b, r["loc"].at[i]) for i, (a, b) in enumerate(copies)]
    for cp in copies:
        cp.start()
    stores = [pltpu.make_async_copy(a, b, r["osem"].at[i]) for i, (a, b) in enumerate(
        [(r["GO"], r["gw_out"]), (r["GI"], r["gw_in"]), (r["OUT"], r["g_in"])])]
    r["store"] = lambda i: stores[i].start()

    tasks, msgs = plan(dims, (z, y, x, c), r)
    order = order_of(tasks, msgs, LOADS)[0]

    barrier = pltpu.get_barrier_semaphore()
    rows = [((z + s + NZ) % NZ) * NY + y for s in (1, -1)] + [z * NY + (y + s + NY) % NY for s in (1, -1)]
    cols = [((x + j) % NX) * 2 + c for j in range(1, NX)] + [x * 2 + 1 - c]
    rows.append(z * NY + (y + 2) % NY)
    peers = [{"row": v} for v in rows] + [{"col": v} for v in cols]
    for dev in peers:
        pl.semaphore_signal(barrier, inc=1, device_id=dev, device_id_type=MESH)
    pl.semaphore_wait(barrier, len(peers))

    def rcopy(m, src, dst, dev):
        return pltpu.make_async_remote_copy(src_ref=src, dst_ref=dst, send_sem=r["ss"].at[m.index],
                                            recv_sem=r["rs"].at[m.index], device_id=dev, device_id_type=MESH)

    started = []
    for t in order:
        for w in t.waits:
            if w[0] == "load":
                copies[w[1]].wait()
            else:
                m = msgs[w]
                region = m.region()
                rcopy(m, region, region, m.make()[2]).wait_recv()
        if t.run is not None:
            t.run()
        for s in t.sends:
            cp = rcopy(msgs[s], *msgs[s].make())
            cp.start()
            started.append(cp)
    for cp in started:
        cp.wait_send()
    for cp in stores:
        cp.wait()


def build(dims):
    NZ, NY, NX, T, W, F, bounds, NA = dims
    HOPS, BT = NZ // 2, NY * T
    XT, FH = BT // NX, F // 2
    AW, BW = bounds[NA], W - bounds[NA]
    QA = max(bounds[i + 1] - bounds[i] for i in range(NA))
    QB = max(bounds[NA + 1] - bounds[NA], W - bounds[NA + 1])

    def body(inputs, hidden_pre, out_grad, weight_in, weight_out):
        any_spec = pl.BlockSpec(memory_space=pl.ANY)
        vm, dma, n = pltpu.VMEM, pltpu.SemaphoreType.DMA, n_msgs(dims)
        return pl.pallas_call(
            functools.partial(kernel, dims),
            out_shape=(
                jax.ShapeDtypeStruct((T, W), BF16),
                jax.ShapeDtypeStruct((W, F), BF16),
                jax.ShapeDtypeStruct((F, W), BF16),
            ),
            in_specs=[any_spec] * 5,
            out_specs=(any_spec,) * 3,
            scratch_shapes=[
                vm((NZ, NY, T, W), BF16),
                vm((NZ, NY, T, W), BF16),
                vm((NZ * BT, F), BF16),
                vm((W, F), BF16),
                vm((F, W), BF16),
                vm((F, NZ * BT), BF16),
                vm((NZ, NX, XT, F), F32),
                vm((NZ, NX, XT, FH), F32),
                vm((NZ, NX, XT, FH), F32),
                vm((NZ, NX - 1, XT, FH), F32),
                vm((NZ, NX, XT, F), BF16),
                vm((NZ, NY, T, W), F32),
                vm((2 * NA * HOPS, NY, T, QA), BF16),
                vm((2 * NA * HOPS, NY, T, QA), BF16),
                vm((NZ, 3, T, BW), BF16),
                vm((NZ, 3, T, BW), BF16),
                vm((NY, T, AW), BF16),
                vm((NY - 1, T, AW), BF16),
                vm((NZ, T, BW), F32),
                vm((2 * NA * HOPS, T, QB), BF16),
                vm((2 * NA * HOPS, T, QB), BF16),
                vm((T, W), BF16),
                vm((W, F), BF16),
                vm((F, W), BF16),
                dma((5,)),
                dma((3,)),
                dma((n,)),
                dma((n,)),
            ],
            compiler_params=pltpu.CompilerParams(
                collective_id=0, has_side_effects=True, vmem_limit_bytes=60 * 2**20
            ),
        )(inputs, hidden_pre, out_grad, weight_in, weight_out)

    return body


def solution(mesh):
    return jax.shard_map(
        build((8, 4, 4, 32, 1536, 768, (0, 256, 384, 512, 640, 1024, 1536), 4)),
        mesh=mesh,
        in_specs=(
            P("row", "col"),
            P(None, "row"),
            P("row", "col"),
            P("col", "row"),
            P("row", "col"),
        ),
        out_specs=(P("row", "col"), P("col", "row"), P("row", "col")),
        check_vma=False,
    )
```

```python
import functools

import jax
import jax.numpy as jnp
from jax import lax
from jax.experimental import pallas as pl
from jax.experimental.pallas import tpu as pltpu
from jax.sharding import PartitionSpec as P

MESH = pl.DeviceIdType.MESH
F32, BF16 = jnp.float32, jnp.bfloat16
NT = (((1,), (1,)), ((), ()))
TN = (((0,), (0,)), ((), ()))
NN = (((1,), (0,)), ((), ()))
NTILE = 256
PTILE = 768
VMEM_MIB = 46
SIGN = (1, -1)

RATE = 45500.0
CORE_RATE = 650000.0
HOP, HOP2 = 2.4, 0.65
CORE_HOP = 1.0
PRIO1 = 0.6
GATE_Y, GATE_B = ("Byr", 0, 3, 0), ("arr", 0, 0, 2, 4)
GATE_BY = (("Byr", 0, 4, 0), ("d", 2), ("d", 2), ("ys", 3), ("Byr", 0, 4, 0))
GATHER = ("y", "zB", "zA", "arr", "By", "Byr", "blk")
PRIO = {
    ("arr", 1): 0.4,
    ("By", 1): 5.2,
    ("Byr", 1): 3,
    ("zA", 1): 1.5,
    ("zB", 1): 3,
    ("y", 1): 1.5,
    ("rzt", False): 0.2,
    ("zB", 0): 0.4,
    "ys": 3,
    "s": 0.7,
    "h": 0.4,
    "v": 5.2,
    ("zA", 0): 0.2,
    "sumA": 0.7,
    ("arr", 0): 0.7,
    ("y", 0): 3,
    ("rzt", True): 0.4,
    "f": 0,
    ("Byr", 0): 1.5,
    ("By", 0): 0.7,
    "d": 0,
    "p": 0.7,
    "e": 1.5,
    "yc": 1.5,
}


class Task:
    def __init__(self, name, deps=(), waits=(), sends=(), cost=0.05, prio=1, run=None):
        self.name, self.deps, self.waits, self.sends = name, tuple(deps), tuple(waits), tuple(sends)
        self.cost, self.prio, self.run = cost, prio, run


class Msg:
    def __init__(self, name, index, links, nbytes, make, region):
        self.name, self.index, self.links, self.nbytes = name, index, links, nbytes
        self.make, self.region = make, region


def order_of(tasks, msgs, loads):
    free = {}
    arrive = dict(loads)
    done, now, out = {}, 0.0, []
    left = list(tasks)
    while left:
        best, soonest = None, None
        for i, t in enumerate(left):
            if any(d not in done for d in t.deps) or any(w not in arrive for w in t.waits):
                continue
            ready = max([0.0] + [arrive[w] for w in t.waits])
            key = (t.prio, ready, i)
            if ready <= now and (best is None or key < best[0]):
                best = (key, i)
            if soonest is None or ready < soonest[0]:
                soonest = (ready, i)
        if best is None:
            now = max(now, soonest[0])
            continue
        t = left.pop(best[1])
        now += t.cost
        done[t.name] = now
        out.append(t)
        for m in t.sends:
            m = msgs[m]
            if m.links == ("core",):
                start = max(now, free.get("core", 0.0))
                free["core"] = start + m.nbytes / CORE_RATE
                arrive[m.name] = free["core"] + CORE_HOP
            else:
                end = 0.0
                for link in m.links:
                    free[link] = max(now, free.get(link, 0.0)) + m.nbytes / RATE
                    end = max(end, free[link])
                arrive[m.name] = end + HOP + (HOP2 if len(m.links) > 1 else 0.0)
    return out, now, done, arrive, free


def gelu_tanh(h):
    return jnp.tanh(0.7978845608 * (h + 0.044715 * h * h * h))


def plan(dims, pos, r):
    NZ, NY, NX, T, W, F, split, bounds, NA = dims
    NQ = len(bounds) - 1
    z, y, x, c = pos
    HOPS, BT, XT, FH, WH = NZ // 2, NY * T, NY * T // NX, F // 2, W // 2
    tasks, msgs = [], {}

    def task(name, **kw):
        tasks.append(Task(name, **kw))
        return name

    def msg(name, links, nbytes, make, region):
        msgs[name] = Msg(name, len(msgs), links, nbytes, make, region)
        return name

    def qs(q):
        return pl.ds(bounds[q], bounds[q + 1] - bounds[q])

    def qw(q):
        return bounds[q + 1] - bounds[q]

    def mod(v, n):
        return (v + 4 * n) % n

    def zdev(s):
        return {"row": mod(z + s, NZ) * NY + y}

    def ydev(s):
        return {"row": z * NY + mod(y + s, NY)}

    def xdev(s):
        return {"col": mod(x + s, NX) * 2 + c}

    core = {"col": x * 2 + 1 - c}
    zof, yof, xof = (lambda k: mod(z + k, NZ)), (lambda k: mod(y + k, NY)), (lambda k: mod(x + k, NX))
    ZL, YL = ("z+", "z-"), ("y+", "y-")

    def xlinks(j):
        return ("x+",) if j == 1 else ("x-",) if j == NX - 1 else ("x+", "x-")

    A, B = pl.ds(0, bounds[NA]), pl.ds(bounds[NA], W - bounds[NA])
    AW, BW = bounds[NA], W - bounds[NA]
    mid, cut, mid_b = split
    GAA, GBB = pl.ds(0, cut), pl.ds(cut, W - cut)
    QA, QB = tuple(range(NA)), (NA, NA + 1)
    YD = ((1, 0), (3, 1), (2, None))

    def half(v):
        return pl.ds(pl.multiple_of(v * FH, 128), FH)

    def limit(d, q):
        return HOPS if (q % 2 == 0) == (d == 0) else HOPS - 1

    def chains(q):
        return [(d, h) for d in (0, 1) for h in range(1, limit(d, q) + 1)]

    def gather(p, own, buf, gate_y, gate_b, gate_by):
        ld = ("load", p)
        gq, GN = (0, mid, cut, mid_b, W), 2
        width = lambda q: gq[q + 1] - gq[q]
        gs = lambda q: pl.ds(gq[q], width(q))
        for j, d in YD:
            msg(("yo", p, j), YL if d is None else (YL[d],), T * cut * 2,
                lambda j=j: (r[own].at[:, GAA], r[buf].at[z, y, :, GAA], ydev(j)), lambda j=j: r[buf].at[z, yof(-j), :, GAA])
        yo = [("yo", p, j) for j in (1, 3, 2)]
        task(("y", p), deps=gate_y, sends=yo, prio=p * PRIO1)
        for q in range(4):
            for d, h in chains(q):
                s = SIGN[d]
                zb = lambda k, s=s: zof(-s * k)
                if q < GN:
                    pick = lambda b, q=q: r[buf].at[b, :, :, gs(q)]
                else:
                    pick = lambda b, q=q: r[buf].at[b, y, :, gs(q)]
                if h == 1 and q >= GN:
                    make = lambda q=q, s=s, pick=pick: (r[own].at[:, gs(q)], pick(z), zdev(s))
                else:
                    make = lambda h=h, s=s, pick=pick, zb=zb: (pick(zb(h - 1)), pick(zb(h - 1)), zdev(s))
                msg(("gz", p, d, q, h), (ZL[d],), (BT if q < GN else T) * width(q) * 2, make,
                    lambda h=h, pick=pick, zb=zb: pick(zb(h)))
                nxt = [("gz", p, d, q, h + 1)] if h < limit(d, q) else []
                task(("arr", p, d, q, h), waits=[("gz", p, d, q, h)], sends=nxt, prio=0,
                     deps=[("arr", p, d, q, h - 1)] if h > 1 else [("zA", p) if q < GN else ("zB", p)])
        first = lambda qq: [("gz", p, d, q, 1) for q in qq for d in (0, 1) if limit(d, q) >= 1]
        task(("zB", p), deps=gate_b, sends=first((2, 3)), prio=p * PRIO1)
        task(("zA", p), deps=[("y", p)], waits=yo + [ld], sends=first((0, 1)), prio=p * PRIO1)
        for k in range(NZ):
            come = []
            for q in range(4 if k else 0):
                come.append(("arr", p, 1, q, k) if k <= limit(1, q) else ("arr", p, 0, q, NZ - k))
            for d in (0, 1):
                s = SIGN[d]
                msg(("by", p, k, d), (YL[d],), T * (W - cut) * 2,
                    lambda s=s, k=k: (r[buf].at[zof(k), y, :, GBB] if k else r[own].at[:, GBB], r[buf].at[zof(k), y, :, GBB], ydev(s)),
                    lambda s=s, k=k: r[buf].at[zof(k), yof(-s), :, GBB])
                fwd = lambda s, k, cols: r[buf].at[zof(k), yof(-s), :, cols]
                cols = gs(GN + d)
                msg(("byr", p, k, d), (YL[d],), T * width(GN + d) * 2,
                    lambda s=s, k=k, cols=cols, fwd=fwd: (fwd(s, k, cols), fwd(s, k, cols), ydev(s)),
                    lambda k=k, cols=cols: r[buf].at[zof(k), yof(-2), :, cols])
            task(("By", p, k), deps=(come[GN:] if k else [("y", p)]) + gate_by[min(k, NZ - k)],
                 sends=[("by", p, k, 0), ("by", p, k, 1)], prio=p * PRIO1)
            for d in (0, 1):
                task(("Byr", p, k, d), deps=[("By", p, k)], waits=[("by", p, k, d)], sends=[("byr", p, k, d)], prio=p * PRIO1)
            task(("blk", p, k), deps=(come[:GN] if k else [("zA", p)]) + [("Byr", p, k, 0), ("Byr", p, k, 1)],
                 waits=[("byr", p, k, 0), ("byr", p, k, 1)], prio=p * PRIO1)

    gather(0, "grad", "G", [], [], [[]] * (HOPS + 1))
    gather(1, "inp", "I", [GATE_Y], [GATE_B], [[g] for g in GATE_BY])
    for i in range(2, 5):
        task(("ld", i), waits=[("load", i)], cost=0, prio=1)

    def both(k):
        return (k,) if k in (0, HOPS) else (k, NZ - k)

    def dot_d(k):
        zbs = [zof(i) for i in both(k)]
        lhs = jnp.concatenate([r["G"][zb].reshape(BT, W) for zb in zbs], axis=0)
        v = lax.dot_general(lhs, r["WO"][...], NT, preferred_element_type=F32)
        for i, zb in enumerate(zbs):
            r["D"][zb] = v[i * BT:(i + 1) * BT].reshape(NX, XT, F)

    def narrow(k):
        return min(k, NZ - k) >= 2

    def sum_core(k):
        v = r["D"][zof(k), :, :, half(c)] + r["PR"][k]
        r["XS"][k] = v
        if narrow(k):
            r["XB"][k] = v.astype(BF16)

    def make_dh(k):
        v = r["XS"][k, x]
        for j in range(1, NX):
            v = v + (r["XC"][k, j - 1].astype(F32) if narrow(k) else r["XR"][k, j - 1])
        zb = zof(k)
        h = r["H"][pl.ds(pl.multiple_of(zb * BT + x * XT, XT), XT), half(c)].astype(F32)
        t = gelu_tanh(h)
        slope = 0.5 * (1.0 + t) + 0.5 * h * (1.0 - t * t) * 0.7978845608 * (1.0 + 3.0 * 0.044715 * h * h)
        r["DH"][zb, x, :, half(c)] = (v * slope).astype(BF16)

    for k in range(NZ):
        msg(("pair", k), ("core",), BT * FH * 4,
            lambda k=k: (r["D"].at[zof(k), :, :, half(1 - c)], r["PR"].at[k], core), lambda k=k: r["PR"].at[k])
        for j in range(1, NX):
            a, b = ("XB", "XC") if narrow(k) else ("XS", "XR")
            msg(("xs", k, j), xlinks(j), XT * FH * (2 if narrow(k) else 4),
                lambda k=k, j=j, a=a, b=b: (r[a].at[k, xof(j)], r[b].at[k, j - 1], xdev(j)),
                lambda k=k, j=j, b=b: r[b].at[k, j - 1])
            msg(("dh", k, j), xlinks(j), XT * FH * 2,
                lambda k=k, j=j: (r["DH"].at[zof(k), x, :, half(c)], r["DH"].at[zof(k), x, :, half(c)], xdev(j)),
                lambda k=k, j=j: r["DH"].at[zof(k), xof(-j), :, half(c)])
        msg(("df", k), ("core",), BT * FH * 2,
            lambda k=k: (r["DH"].at[zof(k), :, :, half(c)], r["DH"].at[zof(k), :, :, half(c)], core),
            lambda k=k: r["DH"].at[zof(k), :, :, half(1 - c)])
        peers = range(1, NX)
        first = min(k, NZ - k) if k else 0
        if k == first:
            task(("d", k), deps=[("blk", 0, i) for i in both(k)] + [("ld", 3)], sends=[("pair", i) for i in both(k)],
                 cost=0.9, prio=1, run=lambda k=k: dot_d(k))
        task(("s", k), deps=[("d", first)], waits=[("pair", k)], sends=[("xs", k, j) for j in peers], cost=0.15, prio=0.5,
             run=lambda k=k: sum_core(k))
        task(("h", k), deps=[("s", k), ("ld", 2)], waits=[("xs", k, j) for j in peers],
             sends=[("dh", k, j) for j in peers], cost=0.2, prio=0.5, run=lambda k=k: make_dh(k))
        task(("f", k), deps=[("h", k)], waits=[("dh", k, j) for j in peers], sends=[("df", k)], prio=0.5)
        task(("e", k), deps=[("f", k)], waits=[("df", k)], prio=0.5)

    def dot_p(k):
        zbs = [zof(i) for i in both(k)]
        lhs = jnp.concatenate([r["DH"][zb].reshape(BT, F) for zb in zbs], axis=0)
        for n in range(0, W, PTILE):
            v = lax.dot_general(lhs, r["WI"][n:n + PTILE, :], NT, preferred_element_type=F32)
            for i, zb in enumerate(zbs):
                r["PF"][zb, :, :, n:n + PTILE] = v[i * BT:(i + 1) * BT].reshape(NY, T, PTILE)

    def ystage(key, k, qq, dep, cost):
        slot = k
        off = bounds[qq[0]]
        loc = lambda q: pl.ds(bounds[q] - off, qw(q))

        def put(i, who, q, extra=None):
            v = r["PF"][zof(k), yof(who), :, qs(q)]
            if extra is not None:
                v = v + r["YR"][slot, extra, :, loc(q)].astype(F32)
            r["YS"][slot, i, :, loc(q)] = v.astype(BF16)

        for d in (0, 1):
            s, mine, other = SIGN[d], qq[d], qq[1 - d]
            for kind, q, i in (("r", mine, 0), ("n", mine, 1 + d), ("m", other, 1 + d)):
                mk = lambda i=i, q=q, s=s: (r["YS"].at[slot, i, :, loc(q)], r["YR"].at[slot, i, :, loc(q)], ydev(s))
                msg((kind, key, d), (YL[d],), T * qw(q) * 2, mk, lambda i=i, q=q: r["YR"].at[slot, i, :, loc(q)])

        def start():
            for d in (0, 1):
                put(0, 2, qq[d])
                put(1 + d, SIGN[d], qq[1 - d])

        task(("ys", key), deps=dep, sends=[("r", key, 0), ("r", key, 1), ("m", key, 0), ("m", key, 1)], cost=cost,
             prio=0.5, run=start)
        for d in (0, 1):
            task(("yc", key, d), deps=[("ys", key)], waits=[("r", key, d)], sends=[("n", key, d)], prio=0.3,
                 run=lambda d=d: put(1 + d, SIGN[d], qq[d], 0))

        def total():
            w = qw(qq[0]) + qw(qq[1])
            v = r["PF"][zof(k), y, :, pl.ds(off, w)]
            for i in (1, 2):
                v = v + r["YR"][slot, i, :, pl.ds(0, w)].astype(F32)
            return v

        return [(kind, key, d) for kind in ("n", "m") for d in (0, 1)], total

    order = [HOPS]
    for d in range(HOPS - 1, 0, -1):
        order += [d, NZ - d]
    order.append(0)
    tag = lambda q, d, h: (d * NA + q % NA) * HOPS + h - 1

    for q in range(NQ):
        for d, h in chains(q):
            s = SIGN[d]
            bs, br = ("AS", "AR") if q < NA else ("BS", "BR")
            cut = (lambda ref, m, q=q: ref.at[m, :, :, pl.ds(0, qw(q))]) if q < NA else (
                lambda ref, m, q=q: ref.at[m, :, pl.ds(0, qw(q))])
            m = tag(q, d, h)
            msg(("rz", d, q, h), (ZL[d],), (BT if q < NA else T) * qw(q) * 2,
                lambda m=m, s=s, bs=bs, br=br, cut=cut: (cut(r[bs], m), cut(r[br], m), zdev(s)),
                lambda m=m, br=br, cut=cut: cut(r[br], m))

    def step_a(d, q, h):
        v = r["PF"][zof(SIGN[d] * h), :, :, qs(q)]
        if h < limit(d, q):
            v = v + r["AR"][tag(q, d, h + 1), :, :, pl.ds(0, qw(q))].astype(F32)
        r["AS"][tag(q, d, h), :, :, pl.ds(0, qw(q))] = v.astype(BF16)

    def step_b(d, q, h, k):
        v = r["VB"][k, :, pl.ds(bounds[q] - bounds[NA], qw(q))]
        if h < limit(d, q):
            v = v + r["BR"][tag(q, d, h + 1), :, pl.ds(0, qw(q))].astype(F32)
        r["BS"][tag(q, d, h), :, pl.ds(0, qw(q))] = v.astype(BF16)

    for n, k in enumerate(order):
        first = min(k, NZ - k) if k else 0
        if k == first:
            task(("p", k), deps=[("e", i) for i in both(k)] + [("ld", 4)], cost=1.1, prio=1 + 0.01 * n,
                 run=lambda k=k: dot_p(k))
        waits, total = ystage(k, k, QB, [("p", first)], 0.15)

        def hold(k=k, total=total):
            r["VB"][k] = total()

        task(("v", k), deps=[("yc", k, 0), ("yc", k, 1)], waits=waits, cost=0.1, prio=0.4, run=hold)
        for q in range(NQ):
            for d, h in chains(q):
                if (h if d == 0 else NZ - h) != k:
                    continue
                waits = [("rz", d, q, h + 1)] if h < limit(d, q) else []
                dep = [("rzt", d, q, h + 1)] if h < limit(d, q) else []
                if q < NA:
                    task(("rzt", d, q, h), deps=dep + [("p", first)], waits=waits, sends=[("rz", d, q, h)], cost=0.08,
                         prio=0.3, run=lambda d=d, q=q, h=h: step_a(d, q, h))
                else:
                    task(("rzt", d, q, h), deps=dep + [("v", k)], waits=waits, sends=[("rz", d, q, h)], cost=0.05,
                         prio=0.3, run=lambda d=d, q=q, h=h, k=k: step_b(d, q, h, k))

    def last_a():
        for q in QA:
            v = r["PF"][z, :, :, qs(q)]
            for d in (0, 1):
                if limit(d, q) >= 1:
                    v = v + r["AR"][tag(q, d, 1), :, :, pl.ds(0, qw(q))].astype(F32)
            r["PF"][z, :, :, qs(q)] = v
            r["YA"][:, :, qs(q)] = v.astype(BF16)

    lasts = lambda qq: [("rz", d, q, 1) for q in qq for d in (0, 1) if limit(d, q) >= 1]
    sent = lambda qq: [("rzt",) + m[1:] for m in lasts(qq)]
    task("sumA", deps=[("p", 0)] + sent(QA), waits=lasts(QA), sends=[("ya", j) for j in (1, 3, 2)], cost=0.3, prio=0.3, run=last_a)
    for j, d in YD:
        msg(("ya", j), YL if d is None else (YL[d],), T * AW * 2,
            lambda j=j: (r["YA"].at[yof(j)], r["AY"].at[j - 1], ydev(j)), lambda j=j: r["AY"].at[j - 1])

    def out_a():
        v = r["PF"][z, y, :, A]
        for j in (1, 2, 3):
            v = v + r["AY"][j - 1].astype(F32)
        r["OUT"][:, A] = v.astype(BF16)

    task("outA", deps=["sumA"], waits=[("ya", j) for j in (1, 3, 2)], cost=0.1, prio=0.3, run=out_a)

    def out_b():
        for q in QB:
            v = r["VB"][0, :, pl.ds(bounds[q] - bounds[NA], qw(q))]
            for d in (0, 1):
                if limit(d, q) >= 1:
                    v = v + r["BR"][tag(q, d, 1), :, pl.ds(0, qw(q))].astype(F32)
            r["OUT"][:, qs(q)] = v.astype(BF16)

    task("outB", deps=[("v", 0)] + sent(QB), waits=lasts(QB), cost=0.1, prio=0.3, run=out_b)
    task("out", deps=["outA", "outB"], cost=0.05)

    def act_piece(i):
        rows = pl.ds(i * BT, BT)
        h = r["H"][rows, :].astype(F32)
        r["AT"][:, rows] = (0.5 * h * (1.0 + gelu_tanh(h))).astype(BF16).T

    def gwo_piece(n):
        cols = pl.ds(n * NTILE, NTILE)
        rhs = r["G"][:, :, :, cols].reshape(NZ * BT, NTILE)
        r["GO"][:, cols] = lax.dot_general(r["AT"][...], rhs, NN, preferred_element_type=F32).astype(BF16)

    def gwi_piece(n):
        cols = pl.ds(n * NTILE, NTILE)
        lhs = r["I"][:, :, :, cols].reshape(NZ * BT, NTILE)
        rhs = r["DH"][...].reshape(NZ * BT, F)
        r["GI"][cols, :] = lax.dot_general(lhs, rhs, TN, preferred_element_type=F32).astype(BF16)

    for i in range(NZ):
        task(("act", i), deps=[("ld", 2)], cost=0.25, prio=5, run=lambda i=i: act_piece(i))
    for n in range(W // NTILE):
        task(("go", n), deps=[("blk", 0, k) for k in range(NZ)] + [("act", i) for i in range(NZ)], cost=0.6, prio=6,
             run=lambda n=n: gwo_piece(n))
    task("goout", deps=[("go", n) for n in range(W // NTILE)], prio=6)
    for n in range(W // NTILE):
        task(("gi", n), deps=[("blk", 1, k) for k in range(NZ)] + [("e", k) for k in range(NZ)], cost=0.65, prio=7,
             run=lambda n=n: gwi_piece(n))
    task("giout", deps=[("gi", n) for n in range(W // NTILE)], prio=7)
    known = {t.name for t in tasks}
    for t in tasks:
        t.deps = tuple(d for d in t.deps if d in known)
        n = t.name
        kind = n if isinstance(n, str) else n[0]
        if kind in GATHER:
            kind = (kind, n[1])
        elif kind == "rzt":
            kind = (kind, n[2] < NA)
        t.prio = PRIO.get(kind, t.prio)
    return tasks, msgs


@functools.lru_cache(None)
def n_msgs(dims):
    return len(plan(dims, (0, 0, 0, 0), {})[1])


LOADS = {("load", 0): 0.5, ("load", 1): 0.5, ("load", 2): 1.5, ("load", 3): 3.0, ("load", 4): 4.5}
NAMES = ("inp", "hid", "grad", "w_in", "w_out", "OUT", "GI", "GO", "G", "I", "H", "WI", "WO", "AT", "D", "PR", "XS",
         "XR", "XB", "XC", "DH", "PF", "AS", "AR", "YS", "YR", "YA", "AY", "VB", "BS", "BR", "loc", "ss", "rs")


def kernel(dims, *refs):
    NZ, NY, NX = dims[:3]
    r = dict(zip(NAMES, refs, strict=True))
    row, col = lax.axis_index("row"), lax.axis_index("col")
    z, y, x, c = row // NY, row % NY, col // 2, col % 2

    copies = [(r["grad"], r["G"].at[z, y]), (r["inp"], r["I"].at[z, y]), (r["hid"], r["H"]), (r["w_out"], r["WO"]),
              (r["w_in"], r["WI"])]
    copies = [pltpu.make_async_copy(a, b, r["loc"].at[i]) for i, (a, b) in enumerate(copies)]
    for cp in copies:
        cp.start()
    tasks, msgs = plan(dims, (z, y, x, c), r)
    order = order_of(tasks, msgs, LOADS)[0]

    barrier = pltpu.get_barrier_semaphore()
    rows = [((z + s + NZ) % NZ) * NY + y for s in (1, -1)] + [z * NY + (y + s + NY) % NY for s in (1, -1)]
    cols = [((x + j) % NX) * 2 + c for j in range(1, NX)] + [x * 2 + 1 - c]
    rows.append(z * NY + (y + 2) % NY)
    peers = [{"row": v} for v in rows] + [{"col": v} for v in cols]
    for dev in peers:
        pl.semaphore_signal(barrier, inc=1, device_id=dev, device_id_type=MESH)
    pl.semaphore_wait(barrier, len(peers))

    def rcopy(m, src, dst, dev):
        return pltpu.make_async_remote_copy(src_ref=src, dst_ref=dst, send_sem=r["ss"].at[m.index],
                                            recv_sem=r["rs"].at[m.index], device_id=dev, device_id_type=MESH)

    started = []
    for t in order:
        for w in t.waits:
            if w[0] == "load":
                copies[w[1]].wait()
            else:
                m = msgs[w]
                region = m.region()
                rcopy(m, region, region, m.make()[2]).wait_recv()
        if t.run is not None:
            t.run()
        for s in t.sends:
            cp = rcopy(msgs[s], *msgs[s].make())
            cp.start()
            started.append(cp)
    for cp in started:
        cp.wait_send()


def store(*refs):
    copies = [pltpu.make_async_copy(refs[i], refs[3 + i], refs[6].at[i]) for i in range(3)]
    for cp in copies:
        cp.start()
    for cp in copies:
        cp.wait()


def build(dims):
    NZ, NY, NX, T, W, F, split, bounds, NA = dims
    HOPS, BT = NZ // 2, NY * T
    XT, FH = BT // NX, F // 2
    AW, BW = bounds[NA], W - bounds[NA]
    QA = max(bounds[i + 1] - bounds[i] for i in range(NA))
    QB = max(bounds[NA + 1] - bounds[NA], W - bounds[NA + 1])

    def body(inputs, hidden_pre, out_grad, weight_in, weight_out):
        any_spec = pl.BlockSpec(memory_space=pl.ANY)
        vm, dma, n = pltpu.VMEM, pltpu.SemaphoreType.DMA, n_msgs(dims)
        shapes = tuple(jax.ShapeDtypeStruct(v, BF16) for v in ((T, W), (W, F), (F, W)))
        outs = pl.pallas_call(
            functools.partial(kernel, dims),
            out_shape=shapes,
            in_specs=[any_spec] * 5,
            out_specs=(pl.BlockSpec(memory_space=pltpu.VMEM),) * 3,
            scratch_shapes=[
                vm((NZ, NY, T, W), BF16),
                vm((NZ, NY, T, W), BF16),
                vm((NZ * BT, F), BF16),
                vm((W, F), BF16),
                vm((F, W), BF16),
                vm((F, NZ * BT), BF16),
                vm((NZ, NX, XT, F), F32),
                vm((NZ, NX, XT, FH), F32),
                vm((NZ, NX, XT, FH), F32),
                vm((NZ, NX - 1, XT, FH), F32),
                vm((NZ, NX, XT, FH), BF16),
                vm((NZ, NX - 1, XT, FH), BF16),
                vm((NZ, NX, XT, F), BF16),
                vm((NZ, NY, T, W), F32),
                vm((2 * NA * HOPS, NY, T, QA), BF16),
                vm((2 * NA * HOPS, NY, T, QA), BF16),
                vm((NZ, 3, T, BW), BF16),
                vm((NZ, 3, T, BW), BF16),
                vm((NY, T, AW), BF16),
                vm((NY - 1, T, AW), BF16),
                vm((NZ, T, BW), F32),
                vm((2 * NA * HOPS, T, QB), BF16),
                vm((2 * NA * HOPS, T, QB), BF16),
                dma((5,)),
                dma((n,)),
                dma((n,)),
            ],
            compiler_params=pltpu.CompilerParams(
                collective_id=0, has_side_effects=True, vmem_limit_bytes=VMEM_MIB * 2**20
            ),
        )(inputs, hidden_pre, out_grad, weight_in, weight_out)
        return pl.pallas_call(
            store,
            out_shape=shapes,
            in_specs=[pl.BlockSpec(memory_space=pltpu.VMEM)] * 3,
            out_specs=(any_spec,) * 3,
            scratch_shapes=[dma((3,))],
            compiler_params=pltpu.CompilerParams(vmem_limit_bytes=8 * 2**20),
        )(*outs)

    return body


def solution(mesh):
    return jax.shard_map(
        build((8, 4, 4, 32, 1536, 768, (256, 512, 1024), (0, 256, 512, 640, 768, 1152, 1536), 4)),
        mesh=mesh,
        in_specs=(
            P("row", "col"),
            P(None, "row"),
            P("row", "col"),
            P("col", "row"),
            P("row", "col"),
        ),
        out_specs=(P("row", "col"), P("col", "row"), P("row", "col")),
        check_vma=False,
    )
```

```python
import functools

import jax
import jax.numpy as jnp
from jax import lax
from jax.experimental import pallas as pl
from jax.experimental.pallas import tpu as pltpu
from jax.sharding import PartitionSpec as P

MESH = pl.DeviceIdType.MESH
F32, BF16 = jnp.float32, jnp.bfloat16
NT = (((1,), (1,)), ((), ()))
TN = (((0,), (0,)), ((), ()))
NN = (((1,), (0,)), ((), ()))
NTILE = 256
PTILE = 768
VMEM_MIB = 46
SIGN = (1, -1)

RATE = 45500.0
CORE_RATE = 650000.0
HOP, HOP2 = 2.4, 0.65
CORE_HOP = 1.0
PRIO1 = 0.6
GATE_Y, GATE_B = ("Byr", 0, 3, 0), ("arr", 0, 0, 2, 4)
GATE_BY = (("Byr", 0, 4, 0), ("d", 2), ("d", 2), ("ys", 3), ("Byr", 0, 4, 0))
GATHER = ("y", "zB", "zA", "arr", "By", "Byr", "blk")
PRIO = {
    ("arr", 1): 0.4,
    ("By", 1): 5.2,
    ("Byr", 1): 3,
    ("zA", 1): 1.5,
    ("zB", 1): 3,
    ("y", 1): 1.5,
    ("rzt", False): 0.2,
    ("zB", 0): 0.4,
    "ys": 3,
    "s": 0.7,
    "h": 0.4,
    "v": 5.2,
    ("zA", 0): 0.2,
    "sumA": 0.7,
    ("arr", 0): 0.7,
    ("y", 0): 3,
    ("rzt", True): 0.4,
    "f": 0,
    ("Byr", 0): 1.5,
    ("By", 0): 0.7,
    "d": 0,
    "p": 0.7,
    "e": 1.5,
    "yc": 1.5,
}


class Task:
    def __init__(self, name, deps=(), waits=(), sends=(), cost=0.05, prio=1, run=None):
        self.name, self.deps, self.waits, self.sends = name, tuple(deps), tuple(waits), tuple(sends)
        self.cost, self.prio, self.run = cost, prio, run


class Msg:
    def __init__(self, name, index, links, nbytes, make, region):
        self.name, self.index, self.links, self.nbytes = name, index, links, nbytes
        self.make, self.region = make, region


def order_of(tasks, msgs, loads):
    free = {}
    arrive = dict(loads)
    done, now, out = {}, 0.0, []
    left = list(tasks)
    while left:
        best, soonest = None, None
        for i, t in enumerate(left):
            if any(d not in done for d in t.deps) or any(w not in arrive for w in t.waits):
                continue
            ready = max([0.0] + [arrive[w] for w in t.waits])
            key = (t.prio, ready, i)
            if ready <= now and (best is None or key < best[0]):
                best = (key, i)
            if soonest is None or ready < soonest[0]:
                soonest = (ready, i)
        if best is None:
            now = max(now, soonest[0])
            continue
        t = left.pop(best[1])
        now += t.cost
        done[t.name] = now
        out.append(t)
        for m in t.sends:
            m = msgs[m]
            if m.links == ("core",):
                start = max(now, free.get("core", 0.0))
                free["core"] = start + m.nbytes / CORE_RATE
                arrive[m.name] = free["core"] + CORE_HOP
            else:
                end = 0.0
                for link in m.links:
                    free[link] = max(now, free.get(link, 0.0)) + m.nbytes / RATE
                    end = max(end, free[link])
                arrive[m.name] = end + HOP + (HOP2 if len(m.links) > 1 else 0.0)
    return out, now, done, arrive, free


def gelu_tanh(h):
    return jnp.tanh(0.7978845608 * (h + 0.044715 * h * h * h))


def plan(dims, pos, r):
    NZ, NY, NX, T, W, F, split, bounds, NA = dims
    NQ = len(bounds) - 1
    z, y, x, c = pos
    HOPS, BT, XT, FH, WH = NZ // 2, NY * T, NY * T // NX, F // 2, W // 2
    tasks, msgs = [], {}

    def task(name, **kw):
        tasks.append(Task(name, **kw))
        return name

    def msg(name, links, nbytes, make, region):
        msgs[name] = Msg(name, len(msgs), links, nbytes, make, region)
        return name

    def qs(q):
        return pl.ds(bounds[q], bounds[q + 1] - bounds[q])

    def qw(q):
        return bounds[q + 1] - bounds[q]

    def mod(v, n):
        return (v + 4 * n) % n

    def zdev(s):
        return {"row": mod(z + s, NZ) * NY + y}

    def ydev(s):
        return {"row": z * NY + mod(y + s, NY)}

    def xdev(s):
        return {"col": mod(x + s, NX) * 2 + c}

    core = {"col": x * 2 + 1 - c}
    zof, yof, xof = (lambda k: mod(z + k, NZ)), (lambda k: mod(y + k, NY)), (lambda k: mod(x + k, NX))
    ZL, YL = ("z+", "z-"), ("y+", "y-")

    def xlinks(j):
        return ("x+",) if j == 1 else ("x-",) if j == NX - 1 else ("x+", "x-")

    A, B = pl.ds(0, bounds[NA]), pl.ds(bounds[NA], W - bounds[NA])
    AW, BW = bounds[NA], W - bounds[NA]
    mid, cut, mid_b = split
    GAA, GBB = pl.ds(0, cut), pl.ds(cut, W - cut)
    QA, QB = tuple(range(NA)), (NA, NA + 1)
    YD = ((1, 0), (3, 1), (2, None))

    def half(v):
        return pl.ds(pl.multiple_of(v * FH, 128), FH)

    def limit(d, q):
        return HOPS if (q % 2 == 0) == (d == 0) else HOPS - 1

    def chains(q):
        return [(d, h) for d in (0, 1) for h in range(1, limit(d, q) + 1)]

    def gather(p, own, buf, gate_y, gate_b, gate_by):
        ld = ("load", p)
        gq, GN = (0, mid, cut, mid_b, W), 2
        width = lambda q: gq[q + 1] - gq[q]
        gs = lambda q: pl.ds(gq[q], width(q))
        for j, d in YD:
            msg(("yo", p, j), YL if d is None else (YL[d],), T * cut * 2,
                lambda j=j: (r[own].at[:, GAA], r[buf].at[z, y, :, GAA], ydev(j)), lambda j=j: r[buf].at[z, yof(-j), :, GAA])
        yo = [("yo", p, j) for j in (1, 3, 2)]
        task(("y", p), deps=gate_y, sends=yo, prio=p * PRIO1)
        for q in range(4):
            for d, h in chains(q):
                s = SIGN[d]
                zb = lambda k, s=s: zof(-s * k)
                if q < GN:
                    pick = lambda b, q=q: r[buf].at[b, :, :, gs(q)]
                else:
                    pick = lambda b, q=q: r[buf].at[b, y, :, gs(q)]
                if h == 1 and q >= GN:
                    make = lambda q=q, s=s, pick=pick: (r[own].at[:, gs(q)], pick(z), zdev(s))
                else:
                    make = lambda h=h, s=s, pick=pick, zb=zb: (pick(zb(h - 1)), pick(zb(h - 1)), zdev(s))
                msg(("gz", p, d, q, h), (ZL[d],), (BT if q < GN else T) * width(q) * 2, make,
                    lambda h=h, pick=pick, zb=zb: pick(zb(h)))
                nxt = [("gz", p, d, q, h + 1)] if h < limit(d, q) else []
                task(("arr", p, d, q, h), waits=[("gz", p, d, q, h)], sends=nxt, prio=0,
                     deps=[("arr", p, d, q, h - 1)] if h > 1 else [("zA", p) if q < GN else ("zB", p)])
        first = lambda qq: [("gz", p, d, q, 1) for q in qq for d in (0, 1) if limit(d, q) >= 1]
        task(("zB", p), deps=gate_b, sends=first((2, 3)), prio=p * PRIO1)
        task(("zA", p), deps=[("y", p)], waits=yo + [ld], sends=first((0, 1)), prio=p * PRIO1)
        for k in range(NZ):
            come = []
            for q in range(4 if k else 0):
                come.append(("arr", p, 1, q, k) if k <= limit(1, q) else ("arr", p, 0, q, NZ - k))
            for d in (0, 1):
                s = SIGN[d]
                msg(("by", p, k, d), (YL[d],), T * (W - cut) * 2,
                    lambda s=s, k=k: (r[buf].at[zof(k), y, :, GBB] if k else r[own].at[:, GBB], r[buf].at[zof(k), y, :, GBB], ydev(s)),
                    lambda s=s, k=k: r[buf].at[zof(k), yof(-s), :, GBB])
                fwd = lambda s, k, cols: r[buf].at[zof(k), yof(-s), :, cols]
                cols = gs(GN + d)
                msg(("byr", p, k, d), (YL[d],), T * width(GN + d) * 2,
                    lambda s=s, k=k, cols=cols, fwd=fwd: (fwd(s, k, cols), fwd(s, k, cols), ydev(s)),
                    lambda k=k, cols=cols: r[buf].at[zof(k), yof(-2), :, cols])
            task(("By", p, k), deps=(come[GN:] if k else [("y", p)]) + gate_by[min(k, NZ - k)],
                 sends=[("by", p, k, 0), ("by", p, k, 1)], prio=p * PRIO1)
            for d in (0, 1):
                task(("Byr", p, k, d), deps=[("By", p, k)], waits=[("by", p, k, d)], sends=[("byr", p, k, d)], prio=p * PRIO1)
            task(("blk", p, k), deps=(come[:GN] if k else [("zA", p)]) + [("Byr", p, k, 0), ("Byr", p, k, 1)],
                 waits=[("byr", p, k, 0), ("byr", p, k, 1)], prio=p * PRIO1)

    gather(0, "grad", "G", [], [], [[]] * (HOPS + 1))
    gather(1, "inp", "I", [GATE_Y], [GATE_B], [[g] for g in GATE_BY])
    for i in range(2, 5):
        task(("ld", i), waits=[("load", i)], cost=0, prio=1)

    def both(k):
        return (k,) if k in (0, HOPS) else (k, NZ - k)

    def dot_d(k):
        zbs = [zof(i) for i in both(k)]
        lhs = jnp.concatenate([r["G"][zb].reshape(BT, W) for zb in zbs], axis=0)
        v = lax.dot_general(lhs, r["WO"][...], NT, preferred_element_type=F32)
        for i, zb in enumerate(zbs):
            r["D"][zb] = v[i * BT:(i + 1) * BT].reshape(NX, XT, F)

    def narrow(k):
        return min(k, NZ - k) >= 2

    def sum_core(k):
        v = r["D"][zof(k), :, :, half(c)] + r["PR"][k]
        r["XS"][k] = v
        if narrow(k):
            r["XB"][k] = v.astype(BF16)

    def make_dh(k):
        v = r["XS"][k, x]
        for j in range(1, NX):
            v = v + (r["XC"][k, j - 1].astype(F32) if narrow(k) else r["XR"][k, j - 1])
        zb = zof(k)
        h = r["H"][pl.ds(pl.multiple_of(zb * BT + x * XT, XT), XT), half(c)].astype(F32)
        t = gelu_tanh(h)
        slope = 0.5 * (1.0 + t) + 0.5 * h * (1.0 - t * t) * 0.7978845608 * (1.0 + 3.0 * 0.044715 * h * h)
        r["DH"][zb, x, :, half(c)] = (v * slope).astype(BF16)

    for k in range(NZ):
        msg(("pair", k), ("core",), BT * FH * 4,
            lambda k=k: (r["D"].at[zof(k), :, :, half(1 - c)], r["PR"].at[k], core), lambda k=k: r["PR"].at[k])
        for j in range(1, NX):
            a, b = ("XB", "XC") if narrow(k) else ("XS", "XR")
            msg(("xs", k, j), xlinks(j), XT * FH * (2 if narrow(k) else 4),
                lambda k=k, j=j, a=a, b=b: (r[a].at[k, xof(j)], r[b].at[k, j - 1], xdev(j)),
                lambda k=k, j=j, b=b: r[b].at[k, j - 1])
            msg(("dh", k, j), xlinks(j), XT * FH * 2,
                lambda k=k, j=j: (r["DH"].at[zof(k), x, :, half(c)], r["DH"].at[zof(k), x, :, half(c)], xdev(j)),
                lambda k=k, j=j: r["DH"].at[zof(k), xof(-j), :, half(c)])
        msg(("df", k), ("core",), BT * FH * 2,
            lambda k=k: (r["DH"].at[zof(k), :, :, half(c)], r["DH"].at[zof(k), :, :, half(c)], core),
            lambda k=k: r["DH"].at[zof(k), :, :, half(1 - c)])
        peers = range(1, NX)
        first = min(k, NZ - k) if k else 0
        if k == first:
            task(("d", k), deps=[("blk", 0, i) for i in both(k)] + [("ld", 3)], sends=[("pair", i) for i in both(k)],
                 cost=0.9, prio=1, run=lambda k=k: dot_d(k))
        task(("s", k), deps=[("d", first)], waits=[("pair", k)], sends=[("xs", k, j) for j in peers], cost=0.15, prio=0.5,
             run=lambda k=k: sum_core(k))
        task(("h", k), deps=[("s", k), ("ld", 2)], waits=[("xs", k, j) for j in peers],
             sends=[("dh", k, j) for j in peers], cost=0.2, prio=0.5, run=lambda k=k: make_dh(k))
        task(("f", k), deps=[("h", k)], waits=[("dh", k, j) for j in peers], sends=[("df", k)], prio=0.5)
        task(("e", k), deps=[("f", k)], waits=[("df", k)], prio=0.5)

    def dot_p(k):
        zbs = [zof(i) for i in both(k)]
        lhs = jnp.concatenate([r["DH"][zb].reshape(BT, F) for zb in zbs], axis=0)
        for n in range(0, W, PTILE):
            v = lax.dot_general(lhs, r["WI"][n:n + PTILE, :], NT, preferred_element_type=F32)
            for i, zb in enumerate(zbs):
                r["PF"][zb, :, :, n:n + PTILE] = v[i * BT:(i + 1) * BT].reshape(NY, T, PTILE)

    def ystage(key, k, qq, dep, cost):
        slot = k
        off = bounds[qq[0]]
        loc = lambda q: pl.ds(bounds[q] - off, qw(q))

        def put(i, who, q, extra=None):
            v = r["PF"][zof(k), yof(who), :, qs(q)]
            if extra is not None:
                v = v + r["YR"][slot, extra, :, loc(q)].astype(F32)
            r["YS"][slot, i, :, loc(q)] = v.astype(BF16)

        for d in (0, 1):
            s, mine, other = SIGN[d], qq[d], qq[1 - d]
            for kind, q, i in (("r", mine, 0), ("n", mine, 1 + d), ("m", other, 1 + d)):
                mk = lambda i=i, q=q, s=s: (r["YS"].at[slot, i, :, loc(q)], r["YR"].at[slot, i, :, loc(q)], ydev(s))
                msg((kind, key, d), (YL[d],), T * qw(q) * 2, mk, lambda i=i, q=q: r["YR"].at[slot, i, :, loc(q)])

        def start():
            for d in (0, 1):
                put(0, 2, qq[d])
                put(1 + d, SIGN[d], qq[1 - d])

        task(("ys", key), deps=dep, sends=[("r", key, 0), ("r", key, 1), ("m", key, 0), ("m", key, 1)], cost=cost,
             prio=0.5, run=start)
        for d in (0, 1):
            task(("yc", key, d), deps=[("ys", key)], waits=[("r", key, d)], sends=[("n", key, d)], prio=0.3,
                 run=lambda d=d: put(1 + d, SIGN[d], qq[d], 0))

        def total():
            w = qw(qq[0]) + qw(qq[1])
            v = r["PF"][zof(k), y, :, pl.ds(off, w)]
            for i in (1, 2):
                v = v + r["YR"][slot, i, :, pl.ds(0, w)].astype(F32)
            return v

        return [(kind, key, d) for kind in ("n", "m") for d in (0, 1)], total

    order = [HOPS]
    for d in range(HOPS - 1, 0, -1):
        order += [d, NZ - d]
    order.append(0)
    tag = lambda q, d, h: (d * NA + q % NA) * HOPS + h - 1

    for q in range(NQ):
        for d, h in chains(q):
            s = SIGN[d]
            bs, br = ("AS", "AR") if q < NA else ("BS", "BR")
            cut = (lambda ref, m, q=q: ref.at[m, :, :, pl.ds(0, qw(q))]) if q < NA else (
                lambda ref, m, q=q: ref.at[m, :, pl.ds(0, qw(q))])
            m = tag(q, d, h)
            msg(("rz", d, q, h), (ZL[d],), (BT if q < NA else T) * qw(q) * 2,
                lambda m=m, s=s, bs=bs, br=br, cut=cut: (cut(r[bs], m), cut(r[br], m), zdev(s)),
                lambda m=m, br=br, cut=cut: cut(r[br], m))

    def step_a(d, q, h):
        v = r["PF"][zof(SIGN[d] * h), :, :, qs(q)]
        if h < limit(d, q):
            v = v + r["AR"][tag(q, d, h + 1), :, :, pl.ds(0, qw(q))].astype(F32)
        r["AS"][tag(q, d, h), :, :, pl.ds(0, qw(q))] = v.astype(BF16)

    def step_b(d, q, h, k):
        v = r["VB"][k, :, pl.ds(bounds[q] - bounds[NA], qw(q))]
        if h < limit(d, q):
            v = v + r["BR"][tag(q, d, h + 1), :, pl.ds(0, qw(q))].astype(F32)
        r["BS"][tag(q, d, h), :, pl.ds(0, qw(q))] = v.astype(BF16)

    for n, k in enumerate(order):
        first = min(k, NZ - k) if k else 0
        if k == first:
            task(("p", k), deps=[("e", i) for i in both(k)] + [("ld", 4)], cost=1.1, prio=1 + 0.01 * n,
                 run=lambda k=k: dot_p(k))
        waits, total = ystage(k, k, QB, [("p", first)], 0.15)

        def hold(k=k, total=total):
            r["VB"][k] = total()

        task(("v", k), deps=[("yc", k, 0), ("yc", k, 1)], waits=waits, cost=0.1, prio=0.4, run=hold)
        for q in range(NQ):
            for d, h in chains(q):
                if (h if d == 0 else NZ - h) != k:
                    continue
                waits = [("rz", d, q, h + 1)] if h < limit(d, q) else []
                dep = [("rzt", d, q, h + 1)] if h < limit(d, q) else []
                if q < NA:
                    task(("rzt", d, q, h), deps=dep + [("p", first)], waits=waits, sends=[("rz", d, q, h)], cost=0.08,
                         prio=0.3, run=lambda d=d, q=q, h=h: step_a(d, q, h))
                else:
                    task(("rzt", d, q, h), deps=dep + [("v", k)], waits=waits, sends=[("rz", d, q, h)], cost=0.05,
                         prio=0.3, run=lambda d=d, q=q, h=h, k=k: step_b(d, q, h, k))

    def last_a():
        for q in QA:
            v = r["PF"][z, :, :, qs(q)]
            for d in (0, 1):
                if limit(d, q) >= 1:
                    v = v + r["AR"][tag(q, d, 1), :, :, pl.ds(0, qw(q))].astype(F32)
            r["PF"][z, :, :, qs(q)] = v
            r["YA"][:, :, qs(q)] = v.astype(BF16)

    lasts = lambda qq: [("rz", d, q, 1) for q in qq for d in (0, 1) if limit(d, q) >= 1]
    sent = lambda qq: [("rzt",) + m[1:] for m in lasts(qq)]
    task("sumA", deps=[("p", 0)] + sent(QA), waits=lasts(QA), sends=[("ya", j) for j in (1, 3, 2)], cost=0.3, prio=0.3, run=last_a)
    for j, d in YD:
        msg(("ya", j), YL if d is None else (YL[d],), T * AW * 2,
            lambda j=j: (r["YA"].at[yof(j)], r["AY"].at[j - 1], ydev(j)), lambda j=j: r["AY"].at[j - 1])

    def out_a():
        v = r["PF"][z, y, :, A]
        for j in (1, 2, 3):
            v = v + r["AY"][j - 1].astype(F32)
        r["OUT"][:, A] = v.astype(BF16)

    task("outA", deps=["sumA"], waits=[("ya", j) for j in (1, 3, 2)], cost=0.1, prio=0.3, run=out_a)

    def out_b():
        for q in QB:
            v = r["VB"][0, :, pl.ds(bounds[q] - bounds[NA], qw(q))]
            for d in (0, 1):
                if limit(d, q) >= 1:
                    v = v + r["BR"][tag(q, d, 1), :, pl.ds(0, qw(q))].astype(F32)
            r["OUT"][:, qs(q)] = v.astype(BF16)

    task("outB", deps=[("v", 0)] + sent(QB), waits=lasts(QB), cost=0.1, prio=0.3, run=out_b)
    task("out", deps=["outA", "outB"], cost=0.05)

    def act_piece(i):
        rows = pl.ds(i * BT, BT)
        h = r["H"][rows, :].astype(F32)
        r["AT"][:, rows] = (0.5 * h * (1.0 + gelu_tanh(h))).astype(BF16).T

    def gwo_piece(n):
        cols = pl.ds(n * NTILE, NTILE)
        rhs = r["G"][:, :, :, cols].reshape(NZ * BT, NTILE)
        r["GO"][:, cols] = lax.dot_general(r["AT"][...], rhs, NN, preferred_element_type=F32).astype(BF16)

    def gwi_piece(n):
        cols = pl.ds(n * NTILE, NTILE)
        lhs = r["I"][:, :, :, cols].reshape(NZ * BT, NTILE)
        rhs = r["DH"][...].reshape(NZ * BT, F)
        r["GI"][cols, :] = lax.dot_general(lhs, rhs, TN, preferred_element_type=F32).astype(BF16)

    for i in range(NZ):
        task(("act", i), deps=[("ld", 2)], cost=0.25, prio=5, run=lambda i=i: act_piece(i))
    for n in range(W // NTILE):
        task(("go", n), deps=[("blk", 0, k) for k in range(NZ)] + [("act", i) for i in range(NZ)], cost=0.6, prio=6,
             run=lambda n=n: gwo_piece(n))
    task("goout", deps=[("go", n) for n in range(W // NTILE)], prio=6)
    for n in range(W // NTILE):
        task(("gi", n), deps=[("blk", 1, k) for k in range(NZ)] + [("e", k) for k in range(NZ)], cost=0.65, prio=7,
             run=lambda n=n: gwi_piece(n))
    task("giout", deps=[("gi", n) for n in range(W // NTILE)], prio=7)
    known = {t.name for t in tasks}
    for t in tasks:
        t.deps = tuple(d for d in t.deps if d in known)
        n = t.name
        kind = n if isinstance(n, str) else n[0]
        if kind in GATHER:
            kind = (kind, n[1])
        elif kind == "rzt":
            kind = (kind, n[2] < NA)
        t.prio = PRIO.get(kind, t.prio)
    return tasks, msgs


@functools.lru_cache(None)
def n_msgs(dims):
    return len(plan(dims, (0, 0, 0, 0), {})[1])


LOADS = {("load", 0): 0.5, ("load", 1): 0.5, ("load", 2): 1.5, ("load", 3): 3.0, ("load", 4): 4.5}
NAMES = ("inp", "hid", "grad", "w_in", "w_out", "OUT", "GI", "GO", "G", "I", "H", "WI", "WO", "AT", "D", "PR", "XS",
         "XR", "XB", "XC", "DH", "PF", "AS", "AR", "YS", "YR", "YA", "AY", "VB", "BS", "BR", "loc", "ss", "rs")


def kernel(dims, *refs):
    NZ, NY, NX = dims[:3]
    r = dict(zip(NAMES, refs, strict=True))
    row, col = lax.axis_index("row"), lax.axis_index("col")
    z, y, x, c = row // NY, row % NY, col // 2, col % 2

    copies = [(r["grad"], r["G"].at[z, y]), (r["inp"], r["I"].at[z, y]), (r["hid"], r["H"]), (r["w_out"], r["WO"]),
              (r["w_in"], r["WI"])]
    copies = [pltpu.make_async_copy(a, b, r["loc"].at[i]) for i, (a, b) in enumerate(copies)]
    for cp in copies:
        cp.start()
    tasks, msgs = plan(dims, (z, y, x, c), r)
    order = order_of(tasks, msgs, LOADS)[0]

    barrier = pltpu.get_barrier_semaphore()
    rows = [((z + s + NZ) % NZ) * NY + y for s in (1, -1)] + [z * NY + (y + s + NY) % NY for s in (1, -1)]
    cols = [((x + j) % NX) * 2 + c for j in range(1, NX)] + [x * 2 + 1 - c]
    rows.append(z * NY + (y + 2) % NY)
    peers = [{"row": v} for v in rows] + [{"col": v} for v in cols]
    for dev in peers:
        pl.semaphore_signal(barrier, inc=1, device_id=dev, device_id_type=MESH)
    pl.semaphore_wait(barrier, len(peers))

    def rcopy(m, src, dst, dev):
        return pltpu.make_async_remote_copy(src_ref=src, dst_ref=dst, send_sem=r["ss"].at[m.index],
                                            recv_sem=r["rs"].at[m.index], device_id=dev, device_id_type=MESH)

    started = []
    for t in order:
        for w in t.waits:
            if w[0] == "load":
                copies[w[1]].wait()
            else:
                m = msgs[w]
                region = m.region()
                rcopy(m, region, region, m.make()[2]).wait_recv()
        if t.run is not None:
            t.run()
        for s in t.sends:
            cp = rcopy(msgs[s], *msgs[s].make())
            cp.start()
            started.append(cp)
    for cp in started:
        cp.wait_send()


def store(*refs):
    copies = [pltpu.make_async_copy(refs[i], refs[3 + i], refs[6].at[i]) for i in range(3)]
    for cp in copies:
        cp.start()
    for cp in copies:
        cp.wait()


def build(dims):
    NZ, NY, NX, T, W, F, split, bounds, NA = dims
    HOPS, BT = NZ // 2, NY * T
    XT, FH = BT // NX, F // 2
    AW, BW = bounds[NA], W - bounds[NA]
    QA = max(bounds[i + 1] - bounds[i] for i in range(NA))
    QB = max(bounds[NA + 1] - bounds[NA], W - bounds[NA + 1])

    def body(inputs, hidden_pre, out_grad, weight_in, weight_out):
        any_spec = pl.BlockSpec(memory_space=pl.ANY)
        vm, dma, n = pltpu.VMEM, pltpu.SemaphoreType.DMA, n_msgs(dims)
        shapes = tuple(jax.ShapeDtypeStruct(v, BF16) for v in ((T, W), (W, F), (F, W)))
        outs = pl.pallas_call(
            functools.partial(kernel, dims),
            out_shape=shapes,
            in_specs=[any_spec] * 5,
            out_specs=(pl.BlockSpec(memory_space=pltpu.VMEM),) * 3,
            scratch_shapes=[
                vm((NZ, NY, T, W), BF16),
                vm((NZ, NY, T, W), BF16),
                vm((NZ * BT, F), BF16),
                vm((W, F), BF16),
                vm((F, W), BF16),
                vm((F, NZ * BT), BF16),
                vm((NZ, NX, XT, F), F32),
                vm((NZ, NX, XT, FH), F32),
                vm((NZ, NX, XT, FH), F32),
                vm((NZ, NX - 1, XT, FH), F32),
                vm((NZ, NX, XT, FH), BF16),
                vm((NZ, NX - 1, XT, FH), BF16),
                vm((NZ, NX, XT, F), BF16),
                vm((NZ, NY, T, W), F32),
                vm((2 * NA * HOPS, NY, T, QA), BF16),
                vm((2 * NA * HOPS, NY, T, QA), BF16),
                vm((NZ, 3, T, BW), BF16),
                vm((NZ, 3, T, BW), BF16),
                vm((NY, T, AW), BF16),
                vm((NY - 1, T, AW), BF16),
                vm((NZ, T, BW), F32),
                vm((2 * NA * HOPS, T, QB), BF16),
                vm((2 * NA * HOPS, T, QB), BF16),
                dma((5,)),
                dma((n,)),
                dma((n,)),
            ],
            compiler_params=pltpu.CompilerParams(
                collective_id=0, has_side_effects=True, vmem_limit_bytes=VMEM_MIB * 2**20
            ),
        )(*(pltpu.with_memory_space_constraint(v, pltpu.MemorySpace.HBM)
            for v in (inputs, hidden_pre, out_grad, weight_in, weight_out)))
        return pl.pallas_call(
            store,
            out_shape=shapes,
            in_specs=[pl.BlockSpec(memory_space=pltpu.VMEM)] * 3,
            out_specs=(any_spec,) * 3,
            scratch_shapes=[dma((3,))],
            compiler_params=pltpu.CompilerParams(vmem_limit_bytes=8 * 2**20),
        )(*outs)

    return body


def solution(mesh):
    return jax.shard_map(
        build((8, 4, 4, 32, 1536, 768, (256, 512, 1024), (0, 256, 512, 640, 768, 1152, 1536), 4)),
        mesh=mesh,
        in_specs=(
            P("row", "col"),
            P(None, "row"),
            P("row", "col"),
            P("col", "row"),
            P("row", "col"),
        ),
        out_specs=(P("row", "col"), P("col", "row"), P("row", "col")),
        check_vma=False,
    )
```

```python
import functools

import jax
import jax.numpy as jnp
from jax import lax
from jax.experimental import pallas as pl
from jax.experimental.pallas import tpu as pltpu
from jax.sharding import PartitionSpec as P

MESH = pl.DeviceIdType.MESH
F32, BF16 = jnp.float32, jnp.bfloat16
NT = (((1,), (1,)), ((), ()))
TN = (((0,), (0,)), ((), ()))
NN = (((1,), (0,)), ((), ()))
NTILE = 256
PTILE = 768
PARTS = (1, 6, 6)
VMEM_MIB = 46
SIGN = (1, -1)

RATE = 45500.0
CORE_RATE = 650000.0
HOP, HOP2 = 2.4, 0.65
CORE_HOP = 1.0
PRIO1 = 0.6
GATE_Y, GATE_B = ("Byr", 0, 3, 0), ("arr", 0, 0, 2, 4)
GATE_BY = (("Byr", 0, 4, 0), ("d", 2), ("d", 2), ("ys", 3), ("Byr", 0, 4, 0))
GATHER = ("y", "zB", "zA", "arr", "By", "Byr", "blk")
PRIO = {
    ("arr", 1): 0.4,
    ("By", 1): 5.2,
    ("Byr", 1): 3,
    ("zA", 1): 1.5,
    ("zB", 1): 3,
    ("y", 1): 1.5,
    ("rzt", False): 0.2,
    ("zB", 0): 0.4,
    "ys": 3,
    "s": 0.7,
    "h": 0.4,
    "v": 5.2,
    ("zA", 0): 0.2,
    "sumA": 0.7,
    ("arr", 0): 0.7,
    ("y", 0): 3,
    ("rzt", True): 0.4,
    "f": 0,
    ("Byr", 0): 1.5,
    ("By", 0): 0.7,
    "d": 0,
    "p": 0.7,
    "e": 1.5,
    "yc": 1.5,
}


class Task:
    def __init__(self, name, deps=(), waits=(), sends=(), cost=0.05, prio=1, run=None):
        self.name, self.deps, self.waits, self.sends = name, tuple(deps), tuple(waits), tuple(sends)
        self.cost, self.prio, self.run = cost, prio, run


class Msg:
    def __init__(self, name, index, links, nbytes, make, region):
        self.name, self.index, self.links, self.nbytes = name, index, links, nbytes
        self.make, self.region = make, region


def order_of(tasks, msgs, loads):
    free = {}
    arrive = dict(loads)
    done, now, out = {}, 0.0, []
    left = list(tasks)
    while left:
        best, soonest = None, None
        for i, t in enumerate(left):
            if any(d not in done for d in t.deps) or any(w not in arrive for w in t.waits):
                continue
            ready = max([0.0] + [arrive[w] for w in t.waits])
            key = (t.prio, ready, i)
            if ready <= now and (best is None or key < best[0]):
                best = (key, i)
            if soonest is None or ready < soonest[0]:
                soonest = (ready, i)
        if best is None:
            now = max(now, soonest[0])
            continue
        t = left.pop(best[1])
        now += t.cost
        done[t.name] = now
        out.append(t)
        for m in t.sends:
            m = msgs[m]
            if m.links == ("core",):
                start = max(now, free.get("core", 0.0))
                free["core"] = start + m.nbytes / CORE_RATE
                arrive[m.name] = free["core"] + CORE_HOP
            else:
                end = 0.0
                for link in m.links:
                    free[link] = max(now, free.get(link, 0.0)) + m.nbytes / RATE
                    end = max(end, free[link])
                arrive[m.name] = end + HOP + (HOP2 if len(m.links) > 1 else 0.0)
    return out, now, done, arrive, free


def gelu_tanh(h):
    return jnp.tanh(0.7978845608 * (h + 0.044715 * h * h * h))


def plan(dims, pos, r):
    NZ, NY, NX, T, W, F, split, bounds, NA = dims
    NQ = len(bounds) - 1
    z, y, x, c = pos
    HOPS, BT, XT, FH, WH = NZ // 2, NY * T, NY * T // NX, F // 2, W // 2
    tasks, msgs = [], {}

    def task(name, **kw):
        tasks.append(Task(name, **kw))
        return name

    def msg(name, links, nbytes, make, region):
        msgs[name] = Msg(name, len(msgs), links, nbytes, make, region)
        return name

    def qs(q):
        return pl.ds(bounds[q], bounds[q + 1] - bounds[q])

    def qw(q):
        return bounds[q + 1] - bounds[q]

    def mod(v, n):
        return (v + 4 * n) % n

    def zdev(s):
        return {"row": mod(z + s, NZ) * NY + y}

    def ydev(s):
        return {"row": z * NY + mod(y + s, NY)}

    def xdev(s):
        return {"col": mod(x + s, NX) * 2 + c}

    core = {"col": x * 2 + 1 - c}
    zof, yof, xof = (lambda k: mod(z + k, NZ)), (lambda k: mod(y + k, NY)), (lambda k: mod(x + k, NX))
    ZL, YL = ("z+", "z-"), ("y+", "y-")

    def xlinks(j):
        return ("x+",) if j == 1 else ("x-",) if j == NX - 1 else ("x+", "x-")

    A, B = pl.ds(0, bounds[NA]), pl.ds(bounds[NA], W - bounds[NA])
    AW, BW = bounds[NA], W - bounds[NA]
    mid, cut, mid_b = split
    GAA, GBB = pl.ds(0, cut), pl.ds(cut, W - cut)
    QA, QB = tuple(range(NA)), (NA, NA + 1)
    YD = ((1, 0), (3, 1), (2, None))

    def half(v):
        return pl.ds(pl.multiple_of(v * FH, 128), FH)

    def limit(d, q):
        return HOPS if (q % 2 == 0) == (d == 0) else HOPS - 1

    def chains(q):
        return [(d, h) for d in (0, 1) for h in range(1, limit(d, q) + 1)]

    def gather(p, own, buf, gate_y, gate_b, gate_by):
        ld = ("load", p)
        gq, GN = (0, mid, cut, mid_b, W), 2
        width = lambda q: gq[q + 1] - gq[q]
        gs = lambda q: pl.ds(gq[q], width(q))
        for j, d in YD:
            msg(("yo", p, j), YL if d is None else (YL[d],), T * cut * 2,
                lambda j=j: (r[own].at[:, GAA], r[buf].at[z, y, :, GAA], ydev(j)), lambda j=j: r[buf].at[z, yof(-j), :, GAA])
        yo = [("yo", p, j) for j in (1, 3, 2)]
        task(("y", p), deps=gate_y, sends=yo, prio=p * PRIO1)
        for q in range(4):
            for d, h in chains(q):
                s = SIGN[d]
                zb = lambda k, s=s: zof(-s * k)
                if q < GN:
                    pick = lambda b, q=q: r[buf].at[b, :, :, gs(q)]
                else:
                    pick = lambda b, q=q: r[buf].at[b, y, :, gs(q)]
                if h == 1 and q >= GN:
                    make = lambda q=q, s=s, pick=pick: (r[own].at[:, gs(q)], pick(z), zdev(s))
                else:
                    make = lambda h=h, s=s, pick=pick, zb=zb: (pick(zb(h - 1)), pick(zb(h - 1)), zdev(s))
                msg(("gz", p, d, q, h), (ZL[d],), (BT if q < GN else T) * width(q) * 2, make,
                    lambda h=h, pick=pick, zb=zb: pick(zb(h)))
                nxt = [("gz", p, d, q, h + 1)] if h < limit(d, q) else []
                task(("arr", p, d, q, h), waits=[("gz", p, d, q, h)], sends=nxt, prio=0,
                     deps=[("arr", p, d, q, h - 1)] if h > 1 else [("zA", p) if q < GN else ("zB", p)])
        first = lambda qq: [("gz", p, d, q, 1) for q in qq for d in (0, 1) if limit(d, q) >= 1]
        task(("zB", p), deps=gate_b, sends=first((2, 3)), prio=p * PRIO1)
        task(("zA", p), deps=[("y", p)], waits=yo + [ld], sends=first((0, 1)), prio=p * PRIO1)
        for k in range(NZ):
            come = []
            for q in range(4 if k else 0):
                come.append(("arr", p, 1, q, k) if k <= limit(1, q) else ("arr", p, 0, q, NZ - k))
            for d in (0, 1):
                s = SIGN[d]
                msg(("by", p, k, d), (YL[d],), T * (W - cut) * 2,
                    lambda s=s, k=k: (r[buf].at[zof(k), y, :, GBB] if k else r[own].at[:, GBB], r[buf].at[zof(k), y, :, GBB], ydev(s)),
                    lambda s=s, k=k: r[buf].at[zof(k), yof(-s), :, GBB])
                fwd = lambda s, k, cols: r[buf].at[zof(k), yof(-s), :, cols]
                cols = gs(GN + d)
                msg(("byr", p, k, d), (YL[d],), T * width(GN + d) * 2,
                    lambda s=s, k=k, cols=cols, fwd=fwd: (fwd(s, k, cols), fwd(s, k, cols), ydev(s)),
                    lambda k=k, cols=cols: r[buf].at[zof(k), yof(-2), :, cols])
            task(("By", p, k), deps=(come[GN:] if k else [("y", p)]) + gate_by[min(k, NZ - k)],
                 sends=[("by", p, k, 0), ("by", p, k, 1)], prio=p * PRIO1)
            for d in (0, 1):
                task(("Byr", p, k, d), deps=[("By", p, k)], waits=[("by", p, k, d)], sends=[("byr", p, k, d)], prio=p * PRIO1)
            task(("blk", p, k), deps=(come[:GN] if k else [("zA", p)]) + [("Byr", p, k, 0), ("Byr", p, k, 1)],
                 waits=[("byr", p, k, 0), ("byr", p, k, 1)], prio=p * PRIO1)

    gather(0, "grad", "G", [], [], [[]] * (HOPS + 1))
    gather(1, "inp", "I", [GATE_Y], [GATE_B], [[g] for g in GATE_BY])
    for i in range(2, 5):
        task(("ld", i), waits=[("load", i)], cost=0, prio=1)

    def both(k):
        return (k,) if k in (0, HOPS) else (k, NZ - k)

    def dot_d(k):
        zbs = [zof(i) for i in both(k)]
        lhs = jnp.concatenate([r["G"][zb].reshape(BT, W) for zb in zbs], axis=0)
        v = lax.dot_general(lhs, r["WO"][...], NT, preferred_element_type=F32)
        for i, zb in enumerate(zbs):
            r["D"][zb] = v[i * BT:(i + 1) * BT].reshape(NX, XT, F)

    def narrow(k):
        return min(k, NZ - k) >= 2

    def sum_core(k):
        v = r["D"][zof(k), :, :, half(c)] + r["PR"][k]
        r["XS"][k] = v
        if narrow(k):
            r["XB"][k] = v.astype(BF16)

    def make_dh(k):
        v = r["XS"][k, x]
        for j in range(1, NX):
            v = v + (r["XC"][k, j - 1].astype(F32) if narrow(k) else r["XR"][k, j - 1])
        zb = zof(k)
        h = r["H"][pl.ds(pl.multiple_of(zb * BT + x * XT, XT), XT), half(c)].astype(F32)
        t = gelu_tanh(h)
        slope = 0.5 * (1.0 + t) + 0.5 * h * (1.0 - t * t) * 0.7978845608 * (1.0 + 3.0 * 0.044715 * h * h)
        r["DH"][zb, x, :, half(c)] = (v * slope).astype(BF16)

    for k in range(NZ):
        msg(("pair", k), ("core",), BT * FH * 4,
            lambda k=k: (r["D"].at[zof(k), :, :, half(1 - c)], r["PR"].at[k], core), lambda k=k: r["PR"].at[k])
        for j in range(1, NX):
            a, b = ("XB", "XC") if narrow(k) else ("XS", "XR")
            msg(("xs", k, j), xlinks(j), XT * FH * (2 if narrow(k) else 4),
                lambda k=k, j=j, a=a, b=b: (r[a].at[k, xof(j)], r[b].at[k, j - 1], xdev(j)),
                lambda k=k, j=j, b=b: r[b].at[k, j - 1])
            msg(("dh", k, j), xlinks(j), XT * FH * 2,
                lambda k=k, j=j: (r["DH"].at[zof(k), x, :, half(c)], r["DH"].at[zof(k), x, :, half(c)], xdev(j)),
                lambda k=k, j=j: r["DH"].at[zof(k), xof(-j), :, half(c)])
        msg(("df", k), ("core",), BT * FH * 2,
            lambda k=k: (r["DH"].at[zof(k), :, :, half(c)], r["DH"].at[zof(k), :, :, half(c)], core),
            lambda k=k: r["DH"].at[zof(k), :, :, half(1 - c)])
        peers = range(1, NX)
        first = min(k, NZ - k) if k else 0
        if k == first:
            task(("d", k), deps=[("blk", 0, i) for i in both(k)] + [("ld", 3)], sends=[("pair", i) for i in both(k)],
                 cost=0.9, prio=1, run=lambda k=k: dot_d(k))
        task(("s", k), deps=[("d", first)], waits=[("pair", k)], sends=[("xs", k, j) for j in peers], cost=0.15, prio=0.5,
             run=lambda k=k: sum_core(k))
        task(("h", k), deps=[("s", k), ("ld", 2)], waits=[("xs", k, j) for j in peers],
             sends=[("dh", k, j) for j in peers], cost=0.2, prio=0.5, run=lambda k=k: make_dh(k))
        task(("f", k), deps=[("h", k)], waits=[("dh", k, j) for j in peers], sends=[("df", k)], prio=0.5)
        task(("e", k), deps=[("f", k)], waits=[("df", k)], prio=0.5)

    def dot_p(k):
        zbs = [zof(i) for i in both(k)]
        lhs = jnp.concatenate([r["DH"][zb].reshape(BT, F) for zb in zbs], axis=0)
        for n in range(0, W, PTILE):
            v = lax.dot_general(lhs, r["WI"][n:n + PTILE, :], NT, preferred_element_type=F32)
            for i, zb in enumerate(zbs):
                r["PF"][zb, :, :, n:n + PTILE] = v[i * BT:(i + 1) * BT].reshape(NY, T, PTILE)

    def ystage(key, k, qq, dep, cost):
        slot = k
        off = bounds[qq[0]]
        loc = lambda q: pl.ds(bounds[q] - off, qw(q))

        def put(i, who, q, extra=None):
            v = r["PF"][zof(k), yof(who), :, qs(q)]
            if extra is not None:
                v = v + r["YR"][slot, extra, :, loc(q)].astype(F32)
            r["YS"][slot, i, :, loc(q)] = v.astype(BF16)

        for d in (0, 1):
            s, mine, other = SIGN[d], qq[d], qq[1 - d]
            for kind, q, i in (("r", mine, 0), ("n", mine, 1 + d), ("m", other, 1 + d)):
                mk = lambda i=i, q=q, s=s: (r["YS"].at[slot, i, :, loc(q)], r["YR"].at[slot, i, :, loc(q)], ydev(s))
                msg((kind, key, d), (YL[d],), T * qw(q) * 2, mk, lambda i=i, q=q: r["YR"].at[slot, i, :, loc(q)])

        def start():
            for d in (0, 1):
                put(0, 2, qq[d])
                put(1 + d, SIGN[d], qq[1 - d])

        task(("ys", key), deps=dep, sends=[("r", key, 0), ("r", key, 1), ("m", key, 0), ("m", key, 1)], cost=cost,
             prio=0.5, run=start)
        for d in (0, 1):
            task(("yc", key, d), deps=[("ys", key)], waits=[("r", key, d)], sends=[("n", key, d)], prio=0.3,
                 run=lambda d=d: put(1 + d, SIGN[d], qq[d], 0))

        def total():
            w = qw(qq[0]) + qw(qq[1])
            v = r["PF"][zof(k), y, :, pl.ds(off, w)]
            for i in (1, 2):
                v = v + r["YR"][slot, i, :, pl.ds(0, w)].astype(F32)
            return v

        return [(kind, key, d) for kind in ("n", "m") for d in (0, 1)], total

    order = [HOPS]
    for d in range(HOPS - 1, 0, -1):
        order += [d, NZ - d]
    order.append(0)
    tag = lambda q, d, h: (d * NA + q % NA) * HOPS + h - 1

    for q in range(NQ):
        for d, h in chains(q):
            s = SIGN[d]
            bs, br = ("AS", "AR") if q < NA else ("BS", "BR")
            cut = (lambda ref, m, q=q: ref.at[m, :, :, pl.ds(0, qw(q))]) if q < NA else (
                lambda ref, m, q=q: ref.at[m, :, pl.ds(0, qw(q))])
            m = tag(q, d, h)
            msg(("rz", d, q, h), (ZL[d],), (BT if q < NA else T) * qw(q) * 2,
                lambda m=m, s=s, bs=bs, br=br, cut=cut: (cut(r[bs], m), cut(r[br], m), zdev(s)),
                lambda m=m, br=br, cut=cut: cut(r[br], m))

    def step_a(d, q, h):
        v = r["PF"][zof(SIGN[d] * h), :, :, qs(q)]
        if h < limit(d, q):
            v = v + r["AR"][tag(q, d, h + 1), :, :, pl.ds(0, qw(q))].astype(F32)
        r["AS"][tag(q, d, h), :, :, pl.ds(0, qw(q))] = v.astype(BF16)

    def step_b(d, q, h, k):
        v = r["VB"][k, :, pl.ds(bounds[q] - bounds[NA], qw(q))]
        if h < limit(d, q):
            v = v + r["BR"][tag(q, d, h + 1), :, pl.ds(0, qw(q))].astype(F32)
        r["BS"][tag(q, d, h), :, pl.ds(0, qw(q))] = v.astype(BF16)

    for n, k in enumerate(order):
        first = min(k, NZ - k) if k else 0
        if k == first:
            task(("p", k), deps=[("e", i) for i in both(k)] + [("ld", 4)], cost=1.1, prio=1 + 0.01 * n,
                 run=lambda k=k: dot_p(k))
        waits, total = ystage(k, k, QB, [("p", first)], 0.15)

        def hold(k=k, total=total):
            r["VB"][k] = total()

        task(("v", k), deps=[("yc", k, 0), ("yc", k, 1)], waits=waits, cost=0.1, prio=0.4, run=hold)
        for q in range(NQ):
            for d, h in chains(q):
                if (h if d == 0 else NZ - h) != k:
                    continue
                waits = [("rz", d, q, h + 1)] if h < limit(d, q) else []
                dep = [("rzt", d, q, h + 1)] if h < limit(d, q) else []
                if q < NA:
                    task(("rzt", d, q, h), deps=dep + [("p", first)], waits=waits, sends=[("rz", d, q, h)], cost=0.08,
                         prio=0.3, run=lambda d=d, q=q, h=h: step_a(d, q, h))
                else:
                    task(("rzt", d, q, h), deps=dep + [("v", k)], waits=waits, sends=[("rz", d, q, h)], cost=0.05,
                         prio=0.3, run=lambda d=d, q=q, h=h, k=k: step_b(d, q, h, k))

    def last_a():
        for q in QA:
            v = r["PF"][z, :, :, qs(q)]
            for d in (0, 1):
                if limit(d, q) >= 1:
                    v = v + r["AR"][tag(q, d, 1), :, :, pl.ds(0, qw(q))].astype(F32)
            r["PF"][z, :, :, qs(q)] = v
            r["YA"][:, :, qs(q)] = v.astype(BF16)

    lasts = lambda qq: [("rz", d, q, 1) for q in qq for d in (0, 1) if limit(d, q) >= 1]
    sent = lambda qq: [("rzt",) + m[1:] for m in lasts(qq)]
    task("sumA", deps=[("p", 0)] + sent(QA), waits=lasts(QA), sends=[("ya", j) for j in (1, 3, 2)], cost=0.3, prio=0.3, run=last_a)
    for j, d in YD:
        msg(("ya", j), YL if d is None else (YL[d],), T * AW * 2,
            lambda j=j: (r["YA"].at[yof(j)], r["AY"].at[j - 1], ydev(j)), lambda j=j: r["AY"].at[j - 1])

    def out_a():
        v = r["PF"][z, y, :, A]
        for j in (1, 2, 3):
            v = v + r["AY"][j - 1].astype(F32)
        r["OUT"][:, A] = v.astype(BF16)

    task("outA", deps=["sumA"], waits=[("ya", j) for j in (1, 3, 2)], cost=0.1, prio=0.3, run=out_a)

    def out_b():
        for q in QB:
            v = r["VB"][0, :, pl.ds(bounds[q] - bounds[NA], qw(q))]
            for d in (0, 1):
                if limit(d, q) >= 1:
                    v = v + r["BR"][tag(q, d, 1), :, pl.ds(0, qw(q))].astype(F32)
            r["OUT"][:, qs(q)] = v.astype(BF16)

    task("outB", deps=[("v", 0)] + sent(QB), waits=lasts(QB), cost=0.1, prio=0.3, run=out_b)
    task("out", deps=["outA", "outB"], cost=0.05)

    def act_piece(i):
        rows = pl.ds(i * BT, BT)
        h = r["H"][rows, :].astype(F32)
        r["AT"][:, rows] = (0.5 * h * (1.0 + gelu_tanh(h))).astype(BF16).T

    def gwo_piece(n):
        cols = pl.ds(n * NTILE, NTILE)
        rhs = r["G"][:, :, :, cols].reshape(NZ * BT, NTILE)
        r["GO"][:, cols] = lax.dot_general(r["AT"][...], rhs, NN, preferred_element_type=F32).astype(BF16)

    def gwi_piece(n):
        cols = pl.ds(n * NTILE, NTILE)
        lhs = r["I"][:, :, :, cols].reshape(NZ * BT, NTILE)
        rhs = r["DH"][...].reshape(NZ * BT, F)
        r["GI"][cols, :] = lax.dot_general(lhs, rhs, TN, preferred_element_type=F32).astype(BF16)

    for i in range(NZ):
        task(("act", i), deps=[("ld", 2)], cost=0.25, prio=5, run=lambda i=i: act_piece(i))
    for n in range(W // NTILE):
        task(("go", n), deps=[("blk", 0, k) for k in range(NZ)] + [("act", i) for i in range(NZ)], cost=0.6, prio=6,
             run=lambda n=n: gwo_piece(n))
    task("goout", deps=[("go", n) for n in range(W // NTILE)], prio=6)
    for n in range(W // NTILE):
        task(("gi", n), deps=[("blk", 1, k) for k in range(NZ)] + [("e", k) for k in range(NZ)], cost=0.65, prio=7,
             run=lambda n=n: gwi_piece(n))
    task("giout", deps=[("gi", n) for n in range(W // NTILE)], prio=7)
    known = {t.name for t in tasks}
    for t in tasks:
        t.deps = tuple(d for d in t.deps if d in known)
        n = t.name
        kind = n if isinstance(n, str) else n[0]
        if kind in GATHER:
            kind = (kind, n[1])
        elif kind == "rzt":
            kind = (kind, n[2] < NA)
        t.prio = PRIO.get(kind, t.prio)
    return tasks, msgs


@functools.lru_cache(None)
def n_msgs(dims):
    return len(plan(dims, (0, 0, 0, 0), {})[1])


LOADS = {("load", 0): 0.5, ("load", 1): 0.5, ("load", 2): 1.5, ("load", 3): 3.0, ("load", 4): 4.5}
NAMES = ("inp", "hid", "grad", "w_in", "w_out", "OUT", "GI", "GO", "G", "I", "H", "WI", "WO", "AT", "D", "PR", "XS",
         "XR", "XB", "XC", "DH", "PF", "AS", "AR", "YS", "YR", "YA", "AY", "VB", "BS", "BR", "loc", "ss", "rs")


def kernel(dims, *refs):
    NZ, NY, NX = dims[:3]
    r = dict(zip(NAMES, refs, strict=True))
    row, col = lax.axis_index("row"), lax.axis_index("col")
    z, y, x, c = row // NY, row % NY, col // 2, col % 2

    copies = [(r["grad"], r["G"].at[z, y]), (r["inp"], r["I"].at[z, y]), (r["hid"], r["H"]), (r["w_out"], r["WO"]),
              (r["w_in"], r["WI"])]
    copies = [pltpu.make_async_copy(a, b, r["loc"].at[i]) for i, (a, b) in enumerate(copies)]
    for cp in copies:
        cp.start()
    tasks, msgs = plan(dims, (z, y, x, c), r)
    order = order_of(tasks, msgs, LOADS)[0]

    barrier = pltpu.get_barrier_semaphore()
    rows = [((z + s + NZ) % NZ) * NY + y for s in (1, -1)] + [z * NY + (y + s + NY) % NY for s in (1, -1)]
    cols = [((x + j) % NX) * 2 + c for j in range(1, NX)] + [x * 2 + 1 - c]
    rows.append(z * NY + (y + 2) % NY)
    peers = [{"row": v} for v in rows] + [{"col": v} for v in cols]
    for dev in peers:
        pl.semaphore_signal(barrier, inc=1, device_id=dev, device_id_type=MESH)
    pl.semaphore_wait(barrier, len(peers))

    def rcopy(m, src, dst, dev):
        return pltpu.make_async_remote_copy(src_ref=src, dst_ref=dst, send_sem=r["ss"].at[m.index],
                                            recv_sem=r["rs"].at[m.index], device_id=dev, device_id_type=MESH)

    started = []
    for t in order:
        for w in t.waits:
            if w[0] == "load":
                copies[w[1]].wait()
            else:
                m = msgs[w]
                region = m.region()
                rcopy(m, region, region, m.make()[2]).wait_recv()
        if t.run is not None:
            t.run()
        for s in t.sends:
            cp = rcopy(msgs[s], *msgs[s].make())
            cp.start()
            started.append(cp)
    for cp in started:
        cp.wait_send()


def store(*refs):
    copies = []
    for i in range(3):
        step = refs[i].shape[0] // PARTS[i]
        for n in range(PARTS[i]):
            rows = pl.ds(n * step, step)
            copies.append(pltpu.make_async_copy(refs[i].at[rows], refs[3 + i].at[rows], refs[6].at[len(copies)]))
    for cp in copies:
        cp.start()
    for cp in copies:
        cp.wait()


def build(dims):
    NZ, NY, NX, T, W, F, split, bounds, NA = dims
    HOPS, BT = NZ // 2, NY * T
    XT, FH = BT // NX, F // 2
    AW, BW = bounds[NA], W - bounds[NA]
    QA = max(bounds[i + 1] - bounds[i] for i in range(NA))
    QB = max(bounds[NA + 1] - bounds[NA], W - bounds[NA + 1])

    def body(inputs, hidden_pre, out_grad, weight_in, weight_out):
        any_spec = pl.BlockSpec(memory_space=pl.ANY)
        vm, dma, n = pltpu.VMEM, pltpu.SemaphoreType.DMA, n_msgs(dims)
        shapes = tuple(jax.ShapeDtypeStruct(v, BF16) for v in ((T, W), (W, F), (F, W)))
        outs = pl.pallas_call(
            functools.partial(kernel, dims),
            out_shape=shapes,
            in_specs=[any_spec] * 5,
            out_specs=(pl.BlockSpec(memory_space=pltpu.VMEM),) * 3,
            scratch_shapes=[
                vm((NZ, NY, T, W), BF16),
                vm((NZ, NY, T, W), BF16),
                vm((NZ * BT, F), BF16),
                vm((W, F), BF16),
                vm((F, W), BF16),
                vm((F, NZ * BT), BF16),
                vm((NZ, NX, XT, F), F32),
                vm((NZ, NX, XT, FH), F32),
                vm((NZ, NX, XT, FH), F32),
                vm((NZ, NX - 1, XT, FH), F32),
                vm((NZ, NX, XT, FH), BF16),
                vm((NZ, NX - 1, XT, FH), BF16),
                vm((NZ, NX, XT, F), BF16),
                vm((NZ, NY, T, W), F32),
                vm((2 * NA * HOPS, NY, T, QA), BF16),
                vm((2 * NA * HOPS, NY, T, QA), BF16),
                vm((NZ, 3, T, BW), BF16),
                vm((NZ, 3, T, BW), BF16),
                vm((NY, T, AW), BF16),
                vm((NY - 1, T, AW), BF16),
                vm((NZ, T, BW), F32),
                vm((2 * NA * HOPS, T, QB), BF16),
                vm((2 * NA * HOPS, T, QB), BF16),
                dma((5,)),
                dma((n,)),
                dma((n,)),
            ],
            compiler_params=pltpu.CompilerParams(
                collective_id=0, has_side_effects=True, vmem_limit_bytes=VMEM_MIB * 2**20
            ),
        )(*(pltpu.with_memory_space_constraint(v, pltpu.MemorySpace.HBM)
            for v in (inputs, hidden_pre, out_grad, weight_in, weight_out)))
        return pl.pallas_call(
            store,
            out_shape=shapes,
            in_specs=[pl.BlockSpec(memory_space=pltpu.VMEM)] * 3,
            out_specs=(any_spec,) * 3,
            scratch_shapes=[dma((sum(PARTS),))],
            compiler_params=pltpu.CompilerParams(vmem_limit_bytes=8 * 2**20),
        )(*outs)

    return body


def solution(mesh):
    return jax.shard_map(
        build((8, 4, 4, 32, 1536, 768, (256, 512, 1024), (0, 256, 512, 640, 768, 1152, 1536), 4)),
        mesh=mesh,
        in_specs=(
            P("row", "col"),
            P(None, "row"),
            P("row", "col"),
            P("col", "row"),
            P("row", "col"),
        ),
        out_specs=(P("row", "col"), P("col", "row"), P("row", "col")),
        check_vma=False,
    )
```
